32 devices in a mesh: dp: 8 (over y, x, core), seq: 4 (over z).
Axes of the slice: x: 2, y: 2, z: 4, core: 2. Of those that a mesh axis runs over, the one named last changes fastest.
Arguments:
- inputs: bfloat16 [8, 3072, 768], P('dp', 'seq'), may hold values from -6 to 6
- pass_embed: bfloat16 [768], P('dp'), may hold values from -3 to 3
- gain_attend: bfloat16 [768], P('dp'), may hold values from 0.25 to 1.75
- shift_attend: bfloat16 [768], P('dp'), may hold values from -3 to 3
- attend_in: bfloat16 [768, 2304], P('dp'), may hold values from -0.21875 to 0.21875
- attend_out: bfloat16 [768, 768], P('dp'), may hold values from -0.875 to 0.875
- gain_hidden: bfloat16 [768], P('dp'), may hold values from 0.25 to 1.75
- shift_hidden: bfloat16 [768], P('dp'), may hold values from -3 to 3
- hidden_up: bfloat16 [768, 3072], P('dp'), may hold values from -0.21875 to 0.21875
- hidden_down: bfloat16 [3072, 768], P('dp'), may hold values from -0.109375 to 0.109375
- cotangent: bfloat16 [8, 3072, 768], P('dp', 'seq'), may hold values from -6 to 6
Outputs:
- layer_out: bfloat16 [8, 3072, 768], P('dp', 'seq')
- input_grad: float32 [8, 3072, 768], P('dp', 'seq')
- embed_grad: float32 [768], P('dp')
- gain_attend_grad: float32 [768], P('dp')
- shift_attend_grad: float32 [768], P('dp')
- attend_in_grad: float32 [768, 2304], P('dp')
- attend_out_grad: float32 [768, 768], P('dp')
- gain_hidden_grad: float32 [768], P('dp')
- shift_hidden_grad: float32 [768], P('dp')
- hidden_up_grad: float32 [768, 3072], P('dp')
- hidden_down_grad: float32 [3072, 768], P('dp')
The draws below stay inside these ranges and needn't reach their ends.
All inputs are finite; a program needn't handle non-finite values.
Results may differ from the reference program's by a relative error of at most 0.007.
Values may be sent and summed in bfloat16 or wider, within the bound.
No kernel may reach another device: no remote copies, remote signals or barrier semaphores. Data moves between devices by JAX's collectives and lax.ppermute only.
A program may use at most 192 MiB of HBM per device.

```python
import jax
import jax.numpy as jnp
from jax import lax

D = 768
H = 12
HD = 64
FF = 3072
LEN = 3072
BATCH = 8


def strengthened(array, own_key, source, target, parts, factor):
    owner, partner = [(jnp.arange(array.shape[position]) // (array.shape[position] // parts)).reshape([-1 if axis == position else 1 for axis in range(array.ndim)]) for position in (source, target)]
    chosen = jax.random.permutation(own_key, parts)[partner]
    strong = (owner == chosen) | (owner == (partner + parts // 2) % parts)
    return jnp.where(strong, factor * array, array)


def shard_levels(stream_key, dims, shards, least, top_value):
    level = 1.0
    for dim, parts in shards:
        draws = jax.random.uniform(jax.random.fold_in(jax.random.fold_in(stream_key, 6), dim), (parts,), jnp.float32, least / len(shards), top_value / len(shards))
        level = level * jnp.repeat(jnp.exp(draws), dims[dim] // parts).reshape((-1,) + (1,) * (len(dims) - 1 - dim))
    return level


def gaussian(rng, dims, deviation, reach, split=(), kind=jnp.bfloat16):
    values = deviation * jax.random.normal(rng, dims, jnp.float32)
    if split:
        values = values * shard_levels(rng, dims, split, -0.22, 0.18)
    return jnp.clip(values, -reach, reach).astype(kind)


def heavy_noise(rng, dims, width, reach, cuts, heavy, kind=jnp.bfloat16):
    array = width * jax.random.normal(rng, dims, jnp.float32)
    if cuts:
        array = array * shard_levels(rng, dims, cuts, -0.22, 0.18)
    return jnp.clip(strengthened(array, jax.random.fold_in(rng, 3), *heavy), -reach, reach).astype(kind)


def setup_inputs(seed: int = 0) -> dict:
    arg_keys = jax.random.split(jax.random.key(seed), 12)
    return {
        "inputs": gaussian(arg_keys[0], (BATCH, LEN, D), 1.0, 6.0, ((0, 8), (1, 4))),
        "pass_embed": gaussian(arg_keys[1], (D,), 0.5, 3.0, ((0, 8),)),
        "gain_attend": jnp.clip(1.0 + 0.15 * jax.random.normal(arg_keys[2], (D,), jnp.float32), 0.25, 1.75).astype(jnp.bfloat16),
        "shift_attend": gaussian(arg_keys[3], (D,), 0.5, 3.0, ((0, 8),)),
        "attend_in": gaussian(arg_keys[4], (D, 3 * D), D ** -0.5, 0.21875, ((0, 8),)),
        "attend_out": gaussian(arg_keys[5], (D, D), (D // 16) ** -0.5, 0.875, ((0, 8),)),
        "gain_hidden": jnp.clip(1.0 + 0.15 * jax.random.normal(arg_keys[6], (D,), jnp.float32), 0.25, 1.75).astype(jnp.bfloat16),
        "shift_hidden": gaussian(arg_keys[7], (D,), 0.5, 3.0, ((0, 8),)),
        "hidden_up": gaussian(arg_keys[8], (D, FF), D ** -0.5, 0.21875, ((0, 8),)),
        "hidden_down": gaussian(arg_keys[9], (FF, D), FF ** -0.5, 0.109375, ((0, 8),)),
        "cotangent": heavy_noise(arg_keys[10], (BATCH, LEN, D), 1.0, 6.0, ((0, 8), (1, 4)), (0, 2, 8, 2.0)),
    }


@jax.custom_vjp
def low(v):
    return lax.optimization_barrier(v.astype(jnp.bfloat16)).astype(jnp.float32)

@jax.custom_vjp
def low_back(v):
    return v

def low_keep(v):
    return (low(v), None)

def low_pass(kept, grad):
    return (grad,)

def back_keep(v):
    return (v, None)

def back_low(kept, grad):
    return (low(grad),)
low.defvjp(low_keep, low_pass)
low_back.defvjp(back_keep, back_low)
EPSILON = 1e-05
MASKED = -1e+30
HIGH = lax.Precision.HIGHEST

def layer_norm(hidden, gain, shift):
    center = hidden - lax.optimization_barrier(jnp.mean(hidden, axis=-1, keepdims=True))
    spread = lax.optimization_barrier(jnp.mean(center * center, axis=-1, keepdims=True))
    return center * lax.rsqrt(spread + EPSILON) * gain + shift

def matmul(left, right):
    return jnp.dot(left, right, precision=HIGH)

def attend_block(query_blk, keys, values, first_row):
    block_rows = query_blk.shape[0]
    scores = jnp.einsum('qhd,khd->hqk', query_blk, keys, precision=HIGH) * HD ** (-0.5)
    scores = low_back(scores)
    query_pos = first_row + jnp.arange(block_rows, dtype=jnp.int32)
    key_pos = jnp.arange(keys.shape[0], dtype=jnp.int32)
    causal = key_pos[None, :] <= query_pos[:, None]
    scores = jnp.where(causal[None], scores, MASKED)
    row_max = lax.optimization_barrier(jnp.max(scores, axis=-1, keepdims=True))
    raw_weights = jnp.exp(scores - row_max)
    probs = low(raw_weights / lax.optimization_barrier(jnp.sum(raw_weights, axis=-1, keepdims=True)))
    return jnp.einsum('hqk,khd->qhd', probs, values, precision=HIGH)

def attention(queries, keys, values):
    block_rows = min(512, LEN)
    block_count = LEN // block_rows
    blocks = queries.reshape(block_count, block_rows, H, HD)

    def attend_one(pieces):
        query_blk, block_idx = pieces
        return attend_block(query_blk, keys, values, block_idx * block_rows)
    result = lax.map(jax.checkpoint(attend_one), (blocks, jnp.arange(block_count, dtype=jnp.int32)))
    return result.reshape(LEN, D)

def forward(tokens, pass_embed, gain_attend, shift_attend, attend_in, attend_out, gain_hidden, shift_hidden, hidden_up, hidden_down):
    resid_zero = tokens + pass_embed
    normed_one = low(layer_norm(resid_zero, gain_attend, shift_attend))
    packed = low(low_back(matmul(normed_one, attend_in)))
    queries = packed[:, :D].reshape(LEN, H, HD)
    keys = packed[:, D:2 * D].reshape(LEN, H, HD)
    values = packed[:, 2 * D:].reshape(LEN, H, HD)
    attended = low(low_back(attention(queries, keys, values)))
    branch = low_back(matmul(attended, attend_out))
    resid_one = resid_zero + branch
    normed_two = low(layer_norm(resid_one, gain_hidden, shift_hidden))
    pre_act = low_back(matmul(normed_two, hidden_up))
    activated = low(jax.nn.gelu(pre_act, approximate=True))
    return resid_one + matmul(activated, hidden_down)

def reference(inputs, pass_embed, gain_attend, shift_attend, attend_in, attend_out, gain_hidden, shift_hidden, hidden_up, hidden_down, cotangent):
    params = tuple((p.astype(jnp.float32) for p in (pass_embed, gain_attend, shift_attend, attend_in, attend_out, gain_hidden, shift_hidden, hidden_up, hidden_down)))

    def per_sequence(running, pieces):
        tokens, grad_out = pieces
        result, backward = jax.vjp(forward, tokens.astype(jnp.float32), *params)
        grads = backward(grad_out.astype(jnp.float32))
        updated = tuple((acc + grad for acc, grad in zip(running, grads[1:])))
        return (updated, (result.astype(jnp.bfloat16), grads[0]))
    zeros_init = tuple((jnp.zeros_like(p) for p in params))
    totals, (layer_out, input_grad) = lax.scan(per_sequence, zeros_init, (inputs, cotangent))
    return (layer_out, input_grad, totals[0], totals[1], totals[2], totals[3], totals[4], totals[5], totals[6], totals[7], totals[8])
```

```python
import functools

import jax
import jax.numpy as jnp
from jax import lax
from jax.experimental import pallas as pl
from jax.experimental.pallas import tpu as pltpu
from jax.sharding import PartitionSpec as P

HD = 64
EPSILON = 1e-05
MASKED = -1e30
F32 = jnp.float32
BF = jnp.bfloat16
MEMBERS = 4
VMEM_LIMIT = 60 << 20
GELU_A = 0.7978845608028654
GELU_B = 0.044715


def contract(left, right, left_dim, right_dim):
    return lax.dot_general(
        left, right, (((left_dim,), (right_dim,)), ((), ())), preferred_element_type=F32
    )


def normalize(hidden):
    center = hidden - jnp.mean(hidden, axis=-1, keepdims=True)
    spread = jnp.mean(center * center, axis=-1, keepdims=True)
    inverse = lax.rsqrt(spread + EPSILON)
    return center * inverse, inverse


def norm_backward(grad, gain, unit, inverse):
    scaled = grad * gain
    return inverse * (
        scaled
        - jnp.mean(scaled, axis=-1, keepdims=True)
        - unit * jnp.mean(scaled * unit, axis=-1, keepdims=True)
    )


def params(*semantics):
    return pltpu.CompilerParams(dimension_semantics=semantics, vmem_limit_bytes=VMEM_LIMIT)


def whole(shape):
    zeros = (0,) * len(shape)
    return pl.BlockSpec(shape, lambda *_: zeros, pipeline_mode=pl.Buffered(1))


def project_body(info, stay0, move0, stay1, move1, wt, *rest):
    packed, normed = rest[-2:]
    slot = pl.program_id(0)
    stay = info[0] > 0
    tokens = jnp.where(
        slot == 0,
        jnp.where(stay, stay0[...], move0[...]),
        jnp.where(stay, stay1[...], move1[...]),
    )
    width = tokens.shape[1]
    cols = wt.shape[0] - 64
    vec = wt[cols : cols + 8, :].astype(F32)
    hidden = tokens.astype(F32) + vec[0:1]
    unit, _ = normalize(hidden)
    low = (unit * vec[1:2] + vec[2:3]).astype(BF)
    normed[...] = low
    packed[...] = contract(wt[:cols, :], low, 1, 1).astype(BF)


def project(info, stay0, move0, stay1, move1, wt, carried, rows=384):
    chunk, width = stay0.shape
    cols = wt.shape[0] - 64
    length = MEMBERS * chunk
    per = chunk // rows

    def src(which):
        return pl.BlockSpec(
            (rows, width), lambda s, b, info: (jnp.where(s == which, b, which * 0 + (per - 1) * (s > which)), 0)
        )

    def place(s, b, info):
        return info[1 + s] * per + b

    in_specs = [src(0), src(0), src(1), src(1), whole(wt.shape)]
    aliases = {}
    args = [info, stay0, move0, stay1, move1, wt]
    if carried is not None:
        in_specs += [pl.BlockSpec(memory_space=pl.ANY)] * 2
        aliases = {6: 0, 7: 1}
        args += list(carried)
    return pl.pallas_call(
        project_body,
        grid_spec=pltpu.PrefetchScalarGridSpec(
            num_scalar_prefetch=1,
            grid=(2, per),
            in_specs=in_specs,
            out_specs=[
                pl.BlockSpec((cols, rows), lambda s, b, info: (0, place(s, b, info))),
                pl.BlockSpec((rows, width), lambda s, b, info: (place(s, b, info), 0)),
            ],
        ),
        out_shape=[
            jax.ShapeDtypeStruct((cols, length), BF),
            jax.ShapeDtypeStruct((length, width), BF),
        ],
        input_output_aliases=aliases,
        compiler_params=params("arbitrary", "arbitrary"),
        cost_estimate=pl.CostEstimate(
            flops=4 * chunk * width * cols, transcendentals=2 * chunk, bytes_accessed=12 * chunk * width
        ),
        name="norm_project",
    )(*args)


def diagonal(size):
    key = lax.broadcasted_iota(jnp.int32, (size, size), 0)
    query = lax.broadcasted_iota(jnp.int32, (size, size), 1)
    return key <= query


def forward_body(heads, info, packed, out0, out1, out2, out3, logsum, keys):
    step = pl.program_id(0)
    width = heads * HD
    size = out0.shape[1]
    scale = BF(HD**-0.5)

    @pl.when(step == 0)
    def _():
        for h in range(heads):
            keys[h] = packed[width + h * HD : width + (h + 1) * HD, :].T

    first = pl.multiple_of(step * size, size)
    queries = [packed[h * HD : (h + 1) * HD, pl.ds(first, size)] * scale for h in range(heads)]

    def block(start, carry, allowed):
        all_scores = [
            contract(keys[h, pl.ds(start, size), :], queries[h], 1, 0) for h in range(heads)
        ]
        result = []
        for h in range(heads):
            top, total, summed = carry[h]
            scores = all_scores[h]
            if allowed is not None:
                scores = jnp.where(allowed, scores, MASKED)
            new_top = jnp.maximum(top, jnp.max(scores, axis=0, keepdims=True))
            weights = jnp.exp(scores - new_top)
            shrink = jnp.exp(top - new_top)
            total = total * shrink + jnp.sum(weights, axis=0, keepdims=True)
            values = packed[2 * width + h * HD : 2 * width + (h + 1) * HD, pl.ds(start, size)]
            summed = summed * shrink + contract(values, weights.astype(BF), 1, 0)
            result.append((new_top, total, summed))
        return tuple(result)

    begin = tuple(
        (
            jnp.full((1, size), MASKED, F32),
            jnp.zeros((1, size), F32),
            jnp.zeros((HD, size), F32),
        )
        for _ in range(heads)
    )
    carry = lax.fori_loop(
        0, step, lambda j, c: block(pl.multiple_of(j * size, size), c, None), begin
    )
    carry = block(first, carry, diagonal(size))
    place = step ^ info[1]
    for h in range(heads):
        top, total, summed = carry[h]
        logsum[h : h + 1, :] = top + jnp.log(total)
        low = (summed / total).astype(BF)
        for j, out in enumerate((out0, out1, out2, out3)):

            @pl.when(place == j)
            def _(out=out, low=low, h=h):
                out[h * HD : (h + 1) * HD, :] = low


def attend_forward(info, packed):
    cols, length = packed.shape
    heads = cols // (3 * HD)
    width = heads * HD
    size = length // MEMBERS
    part = jax.ShapeDtypeStruct((width, size), BF)
    return pl.pallas_call(
        functools.partial(forward_body, heads),
        grid_spec=pltpu.PrefetchScalarGridSpec(
            num_scalar_prefetch=1,
            grid=(MEMBERS,),
            in_specs=[whole(packed.shape)],
            out_specs=[pl.BlockSpec((width, size), lambda s, info: (0, 0))] * MEMBERS
            + [pl.BlockSpec((8, size), lambda s, info: (0, s))],
            scratch_shapes=[pltpu.VMEM((heads, length, HD), BF)],
        ),
        out_shape=[part] * MEMBERS + [jax.ShapeDtypeStruct((8, length), F32)],
        compiler_params=params("arbitrary"),
        cost_estimate=pl.CostEstimate(
            flops=10 * heads * length * length * HD,
            transcendentals=heads * length * length // 2,
            bytes_accessed=8 * width * length,
        ),
        name="attention_forward",
    )(info, packed)


def backward_body(heads, info, packed, o0, o1, o2, o3, g0, g1, g2, g3, logsum, normed, wt, *rest):
    n0, n1, n2, n3, dw, keys, values, grad_keys, grad_values, out_all, grad_all, dw_sum = rest
    step = pl.program_id(0)
    chunk_id = MEMBERS - 1 - step
    width = heads * HD
    size = n0.shape[0]
    scale = BF(HD**-0.5)

    @pl.when(step == 0)
    def _():
        for h in range(heads):
            keys[h] = packed[width + h * HD : width + (h + 1) * HD, :].T
            values[h] = packed[2 * width + h * HD : 2 * width + (h + 1) * HD, :].T
        grad_keys[...] = jnp.zeros_like(grad_keys)
        grad_values[...] = jnp.zeros_like(grad_values)
        dw_sum[...] = jnp.zeros_like(dw_sum)
        for j, (o, g) in enumerate(((o0, g0), (o1, g1), (o2, g2), (o3, g3))):
            out_all[info[1] ^ j] = o[...]
            grad_all[info[1] ^ j] = g[...]

    first = pl.multiple_of(chunk_id * size, size)
    rows = [slice(h * HD, (h + 1) * HD) for h in range(heads)]
    query_t = [packed[r, pl.ds(first, size)] * scale for r in rows]
    query = [q.T for q in query_t]
    grad_t = [grad_all[chunk_id, r, :] for r in rows]
    grad = [g.T for g in grad_t]
    delta = [
        jnp.sum(g.astype(F32) * out_all[chunk_id, r, :].astype(F32), axis=0, keepdims=True)
        for g, r in zip(grad_t, rows)
    ]
    lse = [logsum[h : h + 1, :] for h in range(heads)]

    def block(start, carry, allowed):
        result = []
        span = pl.ds(start, size)
        for h in range(heads):
            scores = contract(keys[h, span, :], query_t[h], 1, 0)
            grad_probs = contract(values[h, span, :], grad_t[h], 1, 0)
            probs = jnp.exp(scores - lse[h])
            if allowed is not None:
                probs = jnp.where(allowed, probs, 0.0)
            grad_scores = (probs * (grad_probs - delta[h])).astype(BF)
            grad_values[h, span, :] += contract(probs.astype(BF), grad[h], 1, 0)
            grad_keys[h, span, :] += contract(grad_scores, query[h], 1, 0)
            keys_t = packed[width + h * HD : width + (h + 1) * HD, span]
            result.append(carry[h] + contract(keys_t, grad_scores, 1, 0))
        return tuple(result)

    grad_query = tuple(jnp.zeros((HD, size), F32) for _ in range(heads))
    grad_query = lax.fori_loop(
        0, chunk_id, lambda j, c: block(pl.multiple_of(j * size, size), c, None), grad_query
    )
    grad_query = block(first, grad_query, diagonal(size))
    pieces = [(g * HD**-0.5).astype(BF) for g in grad_query]
    pieces += [grad_keys[h, pl.ds(first, size), :].astype(BF).T for h in range(heads)]
    pieces += [grad_values[h, pl.ds(first, size), :].astype(BF).T for h in range(heads)]
    stacked = jnp.concatenate(pieces, axis=0)
    partial = contract(stacked, wt[: 3 * width, :], 0, 0).astype(BF)
    place = chunk_id ^ info[1]
    for j, out in enumerate((n0, n1, n2, n3)):

        @pl.when(place == j)
        def _(out=out):
            out[...] = partial

    dw_sum[...] += contract(stacked, normed[...], 1, 0)

    @pl.when(step == MEMBERS - 1)
    def _():
        dw[...] = dw_sum[...].astype(BF).T


def attend_backward(info, packed, outs, grads, logsum, normed, wt):
    cols, length = packed.shape
    heads = cols // (3 * HD)
    width = heads * HD
    size = length // MEMBERS
    model = normed.shape[1]
    last = MEMBERS - 1
    fixed = pl.BlockSpec((size, model), lambda s, info: (0, 0))
    return pl.pallas_call(
        functools.partial(backward_body, heads),
        grid_spec=pltpu.PrefetchScalarGridSpec(
            num_scalar_prefetch=1,
            grid=(MEMBERS,),
            in_specs=[whole(packed.shape)]
            + [whole((width, size))] * (2 * MEMBERS)
            + [
                pl.BlockSpec((8, size), lambda s, info: (0, last - s)),
                pl.BlockSpec((size, model), lambda s, info: (last - s, 0)),
                whole(wt.shape),
            ],
            out_specs=[fixed] * MEMBERS + [pl.BlockSpec((model, cols), lambda s, info: (0, 0))],
            scratch_shapes=[
                pltpu.VMEM((heads, length, HD), BF),
                pltpu.VMEM((heads, length, HD), BF),
                pltpu.VMEM((heads, length, HD), F32),
                pltpu.VMEM((heads, length, HD), F32),
                pltpu.VMEM((MEMBERS, width, size), BF),
                pltpu.VMEM((MEMBERS, width, size), BF),
                pltpu.VMEM((cols, model), F32),
            ],
        ),
        out_shape=[jax.ShapeDtypeStruct((size, model), BF)] * MEMBERS
        + [jax.ShapeDtypeStruct((model, cols), BF)],
        compiler_params=params("arbitrary"),
        cost_estimate=pl.CostEstimate(
            flops=20 * heads * length * length * HD,
            transcendentals=heads * length * length // 2,
            bytes_accessed=20 * width * length,
        ),
        name="attention_backward",
    )(info, packed, *outs, *grads, logsum, normed, wt)


def hidden_body(
    groups, info, tok_s, tok_m, cot_s, cot_m, m0, m1, m2, m3, vec_ref, *rest
):
    downs, ups, out_w = rest[:groups], rest[groups : 2 * groups], rest[2 * groups]
    outs = rest[2 * groups + 1 :]
    layer_out, act, grad_pre, normed, branch_grad, resid_grad, a0, a1, a2, a3, stats, cot = outs
    step = pl.program_id(0)
    stay = info[0] > 0
    member = info[1]
    vec = vec_ref[0:8, :].astype(F32)
    model = vec.shape[1]
    width = model // MEMBERS

    def square(ref):
        return ref[...].reshape(model, model)

    def out_rows(j):
        start = pl.multiple_of((member ^ j) * width, width)
        if out_w.shape[0] == 1:
            return out_w[0, pl.ds(start, width), :]
        unit = out_w.shape[1]
        return out_w[pl.ds((member ^ j) * (width // unit), width // unit)].reshape(width, model)

    tokens = jnp.where(stay, tok_s[...], tok_m[...]).astype(F32)
    cot_low = jnp.where(stay, cot_s[...], cot_m[...])
    cot[...] = cot_low
    branch_sum = None
    for j, merged in enumerate((m0, m1, m2, m3)):
        part = contract(merged[...], out_rows(j), 0, 0)
        branch_sum = part if branch_sum is None else branch_sum + part
    resid = tokens + vec[0:1] + branch_sum
    unit, inverse = normalize(resid)
    low = (unit * vec[3:4] + vec[4:5]).astype(BF)
    normed[...] = low
    result = None
    grad_n = jnp.zeros_like(resid)
    for k in range(groups):
        span = slice(k * model, (k + 1) * model)
        up, down = square(ups[k]), square(downs[k])
        pre = contract(low, up, 1, 0)
        square_pre = pre * pre
        bend = jnp.tanh(GELU_A * pre * (1.0 + GELU_B * square_pre))
        half = 0.5 + 0.5 * bend
        act_low = (pre * half).astype(BF)
        act[:, span] = act_low
        part = contract(act_low, down, 1, 0)
        result = part if result is None else result + part
        slope = half + 0.5 * pre * (1.0 - bend * bend) * (
            GELU_A * (1.0 + 3.0 * GELU_B * square_pre)
        )
        grad_low = (contract(cot_low, down, 1, 1) * slope).astype(BF)
        grad_pre[:, span] = grad_low
        grad_n = grad_n + contract(grad_low, up, 1, 1)
    layer_out[...] = (resid + result).astype(BF)
    grad_resid = cot_low.astype(F32) + norm_backward(grad_n, vec[3:4], unit, inverse)
    resid_grad[...] = grad_resid
    branch = grad_resid.astype(BF)
    branch_grad[...] = branch
    for j, out in enumerate((a0, a1, a2, a3)):
        out[...] = contract(out_rows(j), branch, 1, 1).astype(BF)

    @pl.when(step == 0)
    def _():
        stats[...] = jnp.zeros_like(stats)

    stats[0:1, :] += jnp.sum(grad_n * unit, axis=0, keepdims=True)
    stats[1:2, :] += jnp.sum(grad_n, axis=0, keepdims=True)


def weight_specs(weights, groups):
    split, height, model = weights.shape
    unit = model // split
    tall = height - (groups + 1) * unit
    one = pl.Buffered(1)
    per = model // tall if tall < model else 1
    if split == 1:
        specs = [
            pl.BlockSpec((1, model, model), lambda s, info, k=k: (0, k, 0), pipeline_mode=one)
            for k in range(2 * groups + 1)
        ]
        return specs
    downs = [
        pl.BlockSpec((per, tall, model), lambda s, info, k=k: (k, 0, 0), pipeline_mode=one)
        for k in range(groups)
    ]
    base = tall // unit
    others = [
        pl.BlockSpec((split, unit, model), lambda s, info, k=k: (0, base + k, 0), pipeline_mode=one)
        for k in range(groups + 1)
    ]
    return downs + others


def hidden_layer(info, tok_s, tok_m, cot_s, cot_m, merged, wt, weights, groups, rows=256):
    size, model = tok_s.shape
    width = model // MEMBERS
    hidden = groups * model
    tok = pl.BlockSpec((rows, model), lambda s, info: (s, 0))
    col = pl.BlockSpec((width, rows), lambda s, info: (0, s))
    wide = pl.BlockSpec((rows, hidden), lambda s, info: (s, 0))
    vec_block = wt.shape[0] // 64 - 1
    n_weights = 2 * groups + 1

    def shaped(shape, dtype):
        return jax.ShapeDtypeStruct(shape, dtype)

    return pl.pallas_call(
        functools.partial(hidden_body, groups),
        grid_spec=pltpu.PrefetchScalarGridSpec(
            num_scalar_prefetch=1,
            grid=(size // rows,),
            in_specs=[tok] * 4
            + [col] * MEMBERS
            + [pl.BlockSpec((64, model), lambda s, info: (vec_block, 0))]
            + weight_specs(weights, groups),
            out_specs=[tok, wide, wide, tok, tok, tok]
            + [col] * MEMBERS
            + [pl.BlockSpec((8, model), lambda s, info: (0, 0)), tok],
        ),
        out_shape=[
            shaped((size, model), BF),
            shaped((size, hidden), BF),
            shaped((size, hidden), BF),
            shaped((size, model), BF),
            shaped((size, model), BF),
            shaped((size, model), F32),
        ]
        + [shaped((width, size), BF)] * MEMBERS
        + [shaped((8, model), F32), shaped((size, model), BF)],
        compiler_params=params("arbitrary"),
        cost_estimate=pl.CostEstimate(
            flops=2 * size * model * (4 * hidden + 2 * model),
            transcendentals=size * hidden,
            bytes_accessed=2 * weights.size + 24 * size * model,
        ),
        name="hidden_layer",
    )(info, tok_s, tok_m, cot_s, cot_m, *merged, wt, *([weights] * n_weights))


def grads_body(groups, info, act, grad_pre, normed, branch, cot, m0, m1, m2, m3, out, stage, sems):
    step = pl.program_id(0)
    slot = step % 2
    member = info[1]
    units = stage.shape[1]
    unit = stage.shape[2]
    model = stage.shape[3]
    split, height, _ = out.shape
    tall = height - (groups + 1) * (model // split)

    def drain(which):
        pltpu.make_async_copy(stage.at[which], stage.at[which], sems.at[which]).wait()

    @pl.when(step >= 2)
    def _():
        drain(slot)

    @pl.when(step < groups)
    def _():
        stage[slot] = contract(act[...], cot[...], 0, 0).astype(BF).reshape(units, unit, model)

    @pl.when(jnp.logical_and(step >= groups, step < 2 * groups))
    def _():
        stage[slot] = (
            contract(normed[...], grad_pre[...], 0, 0).astype(BF).reshape(units, unit, model)
        )

    @pl.when(step == 2 * groups)
    def _():
        share = units // MEMBERS
        for j, merged in enumerate((m0, m1, m2, m3)):
            piece = contract(merged[...], branch[...], 1, 0).astype(BF)
            stage[slot, pl.ds((member ^ j) * share, share)] = piece.reshape(share, unit, model)

    for b in range(units):
        if split == 1:
            row, start = 0, step * model + b * unit
        else:
            per = tall // unit
            flat = step * units + b
            is_down = step < groups
            row = jnp.where(is_down, flat // per, b)
            start = jnp.where(is_down, (flat % per) * unit, tall + (step - groups) * unit)
        start = pl.multiple_of(start, 16)
        pltpu.make_async_copy(
            stage.at[slot, b], out.at[row, pl.ds(start, unit), :], sems.at[slot]
        ).start()

    @pl.when(step == 2 * groups)
    def _():
        drain(1 - slot)
        drain(slot)


def weight_grads(info, act, grad_pre, normed, branch, cot, merged, split, groups):
    size, model = normed.shape
    width = model // MEMBERS
    units = 8
    height = (2 * groups + 1) * (model // split)
    return pl.pallas_call(
        functools.partial(grads_body, groups),
        grid_spec=pltpu.PrefetchScalarGridSpec(
            num_scalar_prefetch=1,
            grid=(2 * groups + 1,),
            in_specs=[
                pl.BlockSpec((size, model), lambda s, info: (0, jnp.minimum(s, groups - 1))),
                pl.BlockSpec(
                    (size, model), lambda s, info: (0, jnp.clip(s - groups, 0, groups - 1))
                ),
                whole((size, model)),
                whole((size, model)),
                whole((size, model)),
            ]
            + [whole((width, size))] * MEMBERS,
            out_specs=pl.BlockSpec(memory_space=pl.ANY),
            scratch_shapes=[
                pltpu.VMEM((2, units, model // units, model), BF),
                pltpu.SemaphoreType.DMA((2,)),
            ],
        ),
        out_shape=jax.ShapeDtypeStruct((split, height, model), BF),
        compiler_params=params("arbitrary"),
        cost_estimate=pl.CostEstimate(
            flops=2 * size * model * model * (2 * groups + 1),
            transcendentals=0,
            bytes_accessed=2 * (2 * groups + 1) * model * (model + size),
        ),
        name="weight_grads",
    )(info, act, grad_pre, normed, branch, cot, *merged)


def final_body(info, tok_s, tok_m, p0, p1, p2, resid_grad, vec_ref, before, out, low, stats):
    step = pl.program_id(0)
    stay = info[0] > 0
    vec = vec_ref[0:8, :].astype(F32)
    tokens = jnp.where(stay, tok_s[...], tok_m[...]).astype(F32)
    unit, inverse = normalize(tokens + vec[0:1])
    grad = p0[...].astype(F32) + p1[...].astype(F32) + p2[...].astype(F32)
    result = resid_grad[...] + norm_backward(grad, vec[1:2], unit, inverse)
    out[...] = result
    low[...] = result.astype(BF)

    @pl.when(step == 0)
    def _():
        stats[...] = before[...]

    stats[2:3, :] += jnp.sum(grad * unit, axis=0, keepdims=True)
    stats[3:4, :] += jnp.sum(grad, axis=0, keepdims=True)
    stats[4:5, :] += jnp.sum(result, axis=0, keepdims=True)


def final_norm(info, tok_s, tok_m, parts, resid_grad, wt, before, rows=256):
    size, model = tok_s.shape
    tok = pl.BlockSpec((rows, model), lambda s, info: (s, 0))
    one = pl.BlockSpec((8, model), lambda s, info: (0, 0))
    vec_block = wt.shape[0] // 64 - 1
    return pl.pallas_call(
        final_body,
        grid_spec=pltpu.PrefetchScalarGridSpec(
            num_scalar_prefetch=1,
            grid=(size // rows,),
            in_specs=[tok] * 6 + [pl.BlockSpec((64, model), lambda s, info: (vec_block, 0)), one],
            out_specs=[tok, tok, one],
        ),
        out_shape=[
            jax.ShapeDtypeStruct((size, model), F32),
            jax.ShapeDtypeStruct((size, model), BF),
            jax.ShapeDtypeStruct((8, model), F32),
        ],
        compiler_params=params("arbitrary"),
        cost_estimate=pl.CostEstimate(
            flops=30 * size * model, transcendentals=size, bytes_accessed=20 * size * model
        ),
        name="final_norm",
    )(info, tok_s, tok_m, *parts, resid_grad, wt, before)


def after(value, *others):
    return lax.optimization_barrier((value, *others))[0]


def on_device(
    groups_dp,
    inputs,
    pass_embed,
    gain_attend,
    shift_attend,
    attend_in,
    attend_out,
    gain_hidden,
    shift_hidden,
    hidden_up,
    hidden_down,
    cotangent,
):
    axes = ("dp", "seq")
    dp = groups_dp
    row = lax.axis_index("dp")
    line = lax.axis_index("seq")
    core = row & 1
    stays = core == (line >> 1)
    member = core * 2 + (line & 1)
    model = inputs.shape[2]
    width = model // MEMBERS
    share = attend_in.shape[0]
    groups = hidden_up.shape[1] // model

    def send(value, target):
        pairs = []
        for d in range(dp):
            for z in range(MEMBERS):
                goal = target(d, z)
                if goal is not None:
                    pairs.append((d * MEMBERS + z, goal[0] * MEMBERS + goal[1]))
        return lax.ppermute(value, axes, pairs)

    def at_home(d, z):
        return (d & 1) == (z >> 1)

    def swap(d, z):
        return None if at_home(d, z) else (d ^ 1, z ^ 2)

    def other_core(d, z):
        return (d ^ 1, z)

    def next_chip(d, z):
        return (d, z ^ 1)

    mine = inputs[0]
    first = send(mine, lambda d, z: (d, z ^ 1) if at_home(d, z) else (d ^ 1, z ^ 2))
    mine_other = send(mine, other_core)
    late = send(first, lambda d, z: None if at_home(d, z) else (d, z ^ 1))
    first_other = send(first, other_core)
    late_other = send(late, other_core)

    columns = attend_in.reshape(share, 3, MEMBERS, width).transpose(2, 0, 1, 3)
    columns = columns.reshape(MEMBERS, share, 3 * width)
    vectors = jnp.stack([pass_embed, gain_attend, shift_attend, gain_hidden, shift_hidden], axis=1)
    vectors = jnp.pad(vectors, ((0, 0), (0, 59)))

    def for_member(which):
        piece = lax.dynamic_index_in_dim(columns, which, 0, keepdims=False)
        return jnp.concatenate([piece, vectors], axis=1)

    gathered = for_member(member)[None]
    received = send(for_member(member ^ 2), other_core)[None]
    bit = 0
    while True:
        upper = ((row >> bit) & 1) == 1
        gathered = jnp.where(
            upper,
            jnp.concatenate([received, gathered]),
            jnp.concatenate([gathered, received]),
        )
        bit += 1
        if (1 << bit) >= dp:
            break
        received = send(gathered, lambda d, z, bit=bit: (d ^ (1 << bit), z))
    wt = gathered.reshape(model, 3 * width + 64).T

    pack = jnp.concatenate(
        [hidden_down]
        + [hidden_up[:, k * model : (k + 1) * model] for k in range(groups)]
        + [attend_out]
    )
    height = pack.shape[0]
    weights = lax.all_gather(pack, "dp", axis=0, tiled=False)
    split = dp if (model // dp) % 96 == 0 else 1
    if split == 1:
        tall = hidden_down.shape[0]
        down = weights[:, :tall].reshape(1, dp * tall, model)
        others = weights[:, tall:].reshape(dp, groups + 1, share, model).transpose(1, 0, 2, 3)
        weights = jnp.concatenate([down, others.reshape(1, -1, model)], axis=1)

    stay_flag = stays.astype(jnp.int32)
    early = jnp.where(stays, member, member ^ 2)
    info = jnp.stack([stay_flag, member, member, member]).astype(jnp.int32)
    info_early = jnp.stack([stay_flag, early, early ^ 1]).astype(jnp.int32)
    info_late = jnp.stack([stay_flag, early ^ 2, early ^ 3]).astype(jnp.int32)
    carried = project(info_early, mine, mine_other, first, first_other, wt, None)
    packed, normed = project(info_late, first_other, first, late_other, late, wt, carried)

    *outs, logsum = attend_forward(info, packed)
    routes = [None, next_chip, other_core, lambda d, z: (d ^ 1, z ^ 1)]
    merged = [outs[0]] + [send(outs[j], routes[j]) for j in (1, 3, 2)]
    merged = [merged[0], merged[1], merged[3], merged[2]]

    grad_mine = cotangent[0]
    grad_moved = send(after(grad_mine, late), swap)
    (
        layer_out,
        act,
        grad_pre,
        normed_two,
        branch,
        resid_grad,
        a0,
        a1,
        a2,
        a3,
        stats,
        cot,
    ) = hidden_layer(
        info, mine, first, grad_mine, grad_moved, merged, wt, weights, groups
    )
    r1 = send(a1, routes[1])
    r3 = send(a3, routes[3])
    r2 = send(a2, routes[2])
    grads = weight_grads(info, act, grad_pre, normed_two, branch, cot, merged, split, groups)
    if split == 1:
        tall = hidden_down.shape[0]
        down = grads[0, : dp * tall].reshape(dp, tall, model)
        others = grads[0, dp * tall :].reshape(groups + 1, dp, share, model).transpose(1, 0, 2, 3)
        grads = jnp.concatenate([down, others.reshape(dp, -1, model)], axis=1)
    reduced = lax.psum_scatter(grads, "dp", scatter_dimension=0, tiled=True)[0]
    total = lax.psum(reduced, "seq").astype(F32)

    layer_moved = send(after(layer_out, r3), swap)
    n0, n1, n2, n3, dw = attend_backward(
        info, packed, outs, [a0, r1, r2, r3], logsum, normed, wt
    )
    c3 = send(n3, other_core)
    c2 = send(n2, other_core)
    partial = (n1.astype(F32) + c3.astype(F32)).astype(BF)
    z1 = send(partial, next_chip)
    input_grad, input_low, stats = final_norm(
        info, mine, first, [n0, c2, z1], resid_grad, wt, stats
    )
    input_moved = send(input_low, swap)

    current = dw.reshape(dp, share, 3 * width)
    bit = dp.bit_length() - 2
    while bit > 0:
        half = current.shape[0] // 2
        upper = ((row >> bit) & 1) == 1
        give = jnp.where(upper, current[:half], current[half:])
        keep = jnp.where(upper, current[half:], current[:half])
        got = send(give, lambda d, z, bit=bit: (d ^ (1 << bit), z))
        current = (keep.astype(F32) + got.astype(F32)).astype(BF)
        bit -= 1
    got = send(current, lambda d, z: (d, z ^ 2))
    current = (current.astype(F32) + got.astype(F32)).astype(BF)
    upper = core == 1
    give = jnp.where(upper, current[0], current[1])
    keep = jnp.where(upper, current[1], current[0])
    got = send(give, other_core)
    pair = jnp.where(upper, jnp.stack([got, keep]), jnp.stack([keep, got]))
    far = send(pair, next_chip)
    odd = (line & 1) == 1
    quad = jnp.where(odd, jnp.stack([far, pair], axis=1), jnp.stack([pair, far], axis=1))
    proj_grad = quad.reshape(MEMBERS, share, 3, width).transpose(1, 2, 0, 3)
    proj_grad = proj_grad.reshape(share, 3 * model).astype(F32)

    for flip in [lambda d, z, b=b: (d ^ (1 << b), z) for b in range(dp.bit_length() - 1)] + [
        lambda d, z: (d, z ^ 1),
        lambda d, z: (d, z ^ 2),
    ]:
        stats = stats + send(stats, flip)
    small = lax.dynamic_slice(stats, (0, row * share), (8, share))

    tall = hidden_down.shape[0]
    down_grad = total[:tall]
    up_grad = jnp.concatenate(
        [total[tall + k * share : tall + (k + 1) * share] for k in range(groups)], axis=1
    )
    out_grad = total[tall + groups * share :]
    return (
        jnp.where(stays, layer_out, layer_moved)[None],
        jnp.where(stays, input_grad, input_moved.astype(F32))[None],
        small[4],
        small[2],
        small[3],
        proj_grad,
        out_grad,
        small[0],
        small[1],
        up_grad,
        down_grad,
    )


def solution(mesh):
    vector, matrix, tokens = P("dp"), P("dp", None), P("dp", "seq", None)
    return jax.shard_map(
        functools.partial(on_device, mesh.shape["dp"]),
        mesh=mesh,
        in_specs=(
            tokens,
            vector,
            vector,
            vector,
            matrix,
            matrix,
            vector,
            vector,
            matrix,
            matrix,
            tokens,
        ),
        out_specs=(
            tokens,
            tokens,
            vector,
            vector,
            vector,
            matrix,
            matrix,
            vector,
            vector,
            matrix,
            matrix,
        ),
        check_vma=False,
    )
```

```python
import functools

import jax
import jax.numpy as jnp
from jax import lax
from jax.experimental import pallas as pl
from jax.experimental.pallas import tpu as pltpu
from jax.sharding import PartitionSpec as P

HD = 64
EPSILON = 1e-05
MASKED = -1e30
F32 = jnp.float32
BF = jnp.bfloat16
MEMBERS = 4
VMEM_LIMIT = 60 << 20
GELU_A = 0.7978845608028654
GELU_B = 0.044715


def contract(left, right, left_dim, right_dim):
    return lax.dot_general(
        left, right, (((left_dim,), (right_dim,)), ((), ())), preferred_element_type=F32
    )


def normalize(hidden):
    center = hidden - jnp.mean(hidden, axis=-1, keepdims=True)
    spread = jnp.mean(center * center, axis=-1, keepdims=True)
    inverse = lax.rsqrt(spread + EPSILON)
    return center * inverse, inverse


def norm_backward(grad, gain, unit, inverse):
    scaled = grad * gain
    return inverse * (
        scaled
        - jnp.mean(scaled, axis=-1, keepdims=True)
        - unit * jnp.mean(scaled * unit, axis=-1, keepdims=True)
    )


def params(*semantics):
    return pltpu.CompilerParams(dimension_semantics=semantics, vmem_limit_bytes=VMEM_LIMIT)


def whole(shape):
    zeros = (0,) * len(shape)
    return pl.BlockSpec(shape, lambda *_: zeros, pipeline_mode=pl.Buffered(1))


def project_body(info, stay0, move0, stay1, move1, wt, *rest):
    packed, normed = rest[-2:]
    slot = pl.program_id(0)
    stay = info[0] > 0
    tokens = jnp.where(
        slot == 0,
        jnp.where(stay, stay0[...], move0[...]),
        jnp.where(stay, stay1[...], move1[...]),
    )
    width = tokens.shape[1]
    cols = wt.shape[0] - 64
    vec = wt[cols : cols + 8, :].astype(F32)
    hidden = tokens.astype(F32) + vec[0:1]
    unit, _ = normalize(hidden)
    low = (unit * vec[1:2] + vec[2:3]).astype(BF)
    normed[...] = low
    packed[...] = contract(wt[:cols, :], low, 1, 1).astype(BF)


def project(info, stay0, move0, stay1, move1, wt, carried, rows=384):
    chunk, width = stay0.shape
    cols = wt.shape[0] - 64
    length = MEMBERS * chunk
    per = chunk // rows

    def src(which, wanted):
        def index(s, b, info):
            block = jnp.where(s == which, b, (per - 1) * (s > which))
            return (jnp.where(info[0] == wanted, block, 0), 0)

        return pl.BlockSpec((rows, width), index)

    def place(s, b, info):
        return info[1 + s] * per + b

    in_specs = [src(0, 1), src(0, 0), src(1, 1), src(1, 0), whole(wt.shape)]
    aliases = {}
    args = [info, stay0, move0, stay1, move1, wt]
    if carried is not None:
        in_specs += [pl.BlockSpec(memory_space=pl.ANY)] * 2
        aliases = {6: 0, 7: 1}
        args += list(carried)
    return pl.pallas_call(
        project_body,
        grid_spec=pltpu.PrefetchScalarGridSpec(
            num_scalar_prefetch=1,
            grid=(2, per),
            in_specs=in_specs,
            out_specs=[
                pl.BlockSpec((cols, rows), lambda s, b, info: (0, place(s, b, info))),
                pl.BlockSpec((rows, width), lambda s, b, info: (place(s, b, info), 0)),
            ],
        ),
        out_shape=[
            jax.ShapeDtypeStruct((cols, length), BF),
            jax.ShapeDtypeStruct((length, width), BF),
        ],
        input_output_aliases=aliases,
        compiler_params=params("arbitrary", "arbitrary"),
        cost_estimate=pl.CostEstimate(
            flops=4 * chunk * width * cols, transcendentals=2 * chunk, bytes_accessed=12 * chunk * width
        ),
        name="norm_project",
    )(*args)


def diagonal(size):
    key = lax.broadcasted_iota(jnp.int32, (size, size), 0)
    query = lax.broadcasted_iota(jnp.int32, (size, size), 1)
    return key <= query


def forward_body(heads, info, packed, out0, out1, out2, out3, logsum, keys):
    step = pl.program_id(0)
    width = heads * HD
    size = out0.shape[1]
    scale = BF(HD**-0.5)

    @pl.when(step == 0)
    def _():
        for h in range(heads):
            keys[h] = packed[width + h * HD : width + (h + 1) * HD, :].T

    first = pl.multiple_of(step * size, size)
    queries = [packed[h * HD : (h + 1) * HD, pl.ds(first, size)] * scale for h in range(heads)]

    def block(start, carry, allowed):
        all_scores = [
            contract(keys[h, pl.ds(start, size), :], queries[h], 1, 0) for h in range(heads)
        ]
        result = []
        for h in range(heads):
            top, total, summed = carry[h]
            scores = all_scores[h]
            if allowed is not None:
                scores = jnp.where(allowed, scores, MASKED)
            new_top = jnp.maximum(top, jnp.max(scores, axis=0, keepdims=True))
            weights = jnp.exp(scores - new_top)
            shrink = jnp.exp(top - new_top)
            total = total * shrink + jnp.sum(weights, axis=0, keepdims=True)
            values = packed[2 * width + h * HD : 2 * width + (h + 1) * HD, pl.ds(start, size)]
            summed = summed * shrink + contract(values, weights.astype(BF), 1, 0)
            result.append((new_top, total, summed))
        return tuple(result)

    begin = tuple(
        (
            jnp.full((1, size), MASKED, F32),
            jnp.zeros((1, size), F32),
            jnp.zeros((HD, size), F32),
        )
        for _ in range(heads)
    )
    carry = lax.fori_loop(
        0, step, lambda j, c: block(pl.multiple_of(j * size, size), c, None), begin
    )
    carry = block(first, carry, diagonal(size))
    place = step ^ info[1]
    for h in range(heads):
        top, total, summed = carry[h]
        logsum[h : h + 1, :] = top + jnp.log(total)
        low = (summed / total).astype(BF)
        for j, out in enumerate((out0, out1, out2, out3)):

            @pl.when(place == j)
            def _(out=out, low=low, h=h):
                out[h * HD : (h + 1) * HD, :] = low


def attend_forward(info, packed):
    cols, length = packed.shape
    heads = cols // (3 * HD)
    width = heads * HD
    size = length // MEMBERS
    part = jax.ShapeDtypeStruct((width, size), BF)
    return pl.pallas_call(
        functools.partial(forward_body, heads),
        grid_spec=pltpu.PrefetchScalarGridSpec(
            num_scalar_prefetch=1,
            grid=(MEMBERS,),
            in_specs=[whole(packed.shape)],
            out_specs=[pl.BlockSpec((width, size), lambda s, info: (0, 0))] * MEMBERS
            + [pl.BlockSpec((8, size), lambda s, info: (0, s))],
            scratch_shapes=[pltpu.VMEM((heads, length, HD), BF)],
        ),
        out_shape=[part] * MEMBERS + [jax.ShapeDtypeStruct((8, length), F32)],
        compiler_params=params("arbitrary"),
        cost_estimate=pl.CostEstimate(
            flops=10 * heads * length * length * HD,
            transcendentals=heads * length * length // 2,
            bytes_accessed=8 * width * length,
        ),
        name="attention_forward",
    )(info, packed)


def backward_body(heads, info, packed, o0, o1, o2, o3, g0, g1, g2, g3, logsum, normed, wt, *rest):
    n0, n1, n2, n3, dw, keys, values, grad_keys, grad_values, out_all, grad_all, dw_sum = rest
    step = pl.program_id(0)
    chunk_id = MEMBERS - 1 - step
    width = heads * HD
    size = n0.shape[0]
    scale = BF(HD**-0.5)

    @pl.when(step == 0)
    def _():
        for h in range(heads):
            keys[h] = packed[width + h * HD : width + (h + 1) * HD, :].T
            values[h] = packed[2 * width + h * HD : 2 * width + (h + 1) * HD, :].T
        grad_keys[...] = jnp.zeros_like(grad_keys)
        grad_values[...] = jnp.zeros_like(grad_values)
        dw_sum[...] = jnp.zeros_like(dw_sum)
        for j, (o, g) in enumerate(((o0, g0), (o1, g1), (o2, g2), (o3, g3))):
            out_all[info[1] ^ j] = o[...]
            grad_all[info[1] ^ j] = g[...]

    first = pl.multiple_of(chunk_id * size, size)
    rows = [slice(h * HD, (h + 1) * HD) for h in range(heads)]
    query_t = [packed[r, pl.ds(first, size)] * scale for r in rows]
    query = [q.T for q in query_t]
    grad_t = [grad_all[chunk_id, r, :] for r in rows]
    grad = [g.T for g in grad_t]
    delta = [
        jnp.sum(g.astype(F32) * out_all[chunk_id, r, :].astype(F32), axis=0, keepdims=True)
        for g, r in zip(grad_t, rows)
    ]
    lse = [logsum[h : h + 1, :] for h in range(heads)]

    def block(start, carry, allowed):
        result = []
        span = pl.ds(start, size)
        for h in range(heads):
            scores = contract(keys[h, span, :], query_t[h], 1, 0)
            grad_probs = contract(values[h, span, :], grad_t[h], 1, 0)
            probs = jnp.exp(scores - lse[h])
            if allowed is not None:
                probs = jnp.where(allowed, probs, 0.0)
            grad_scores = (probs * (grad_probs - delta[h])).astype(BF)
            grad_values[h, span, :] += contract(probs.astype(BF), grad[h], 1, 0)
            grad_keys[h, span, :] += contract(grad_scores, query[h], 1, 0)
            keys_t = packed[width + h * HD : width + (h + 1) * HD, span]
            result.append(carry[h] + contract(keys_t, grad_scores, 1, 0))
        return tuple(result)

    grad_query = tuple(jnp.zeros((HD, size), F32) for _ in range(heads))
    grad_query = lax.fori_loop(
        0, chunk_id, lambda j, c: block(pl.multiple_of(j * size, size), c, None), grad_query
    )
    grad_query = block(first, grad_query, diagonal(size))
    pieces = [(g * HD**-0.5).astype(BF) for g in grad_query]
    pieces += [grad_keys[h, pl.ds(first, size), :].astype(BF).T for h in range(heads)]
    pieces += [grad_values[h, pl.ds(first, size), :].astype(BF).T for h in range(heads)]
    stacked = jnp.concatenate(pieces, axis=0)
    partial = contract(stacked, wt[: 3 * width, :], 0, 0).astype(BF)
    place = chunk_id ^ info[1]
    for j, out in enumerate((n0, n1, n2, n3)):

        @pl.when(place == j)
        def _(out=out):
            out[...] = partial

    dw_sum[...] += contract(stacked, normed[...], 1, 0)

    @pl.when(step == MEMBERS - 1)
    def _():
        dw[...] = dw_sum[...].astype(BF).T


def attend_backward(info, packed, outs, grads, logsum, normed, wt):
    cols, length = packed.shape
    heads = cols // (3 * HD)
    width = heads * HD
    size = length // MEMBERS
    model = normed.shape[1]
    last = MEMBERS - 1
    fixed = pl.BlockSpec((size, model), lambda s, info: (0, 0))
    return pl.pallas_call(
        functools.partial(backward_body, heads),
        grid_spec=pltpu.PrefetchScalarGridSpec(
            num_scalar_prefetch=1,
            grid=(MEMBERS,),
            in_specs=[whole(packed.shape)]
            + [whole((width, size))] * (2 * MEMBERS)
            + [
                pl.BlockSpec((8, size), lambda s, info: (0, last - s)),
                pl.BlockSpec((size, model), lambda s, info: (last - s, 0)),
                whole(wt.shape),
            ],
            out_specs=[fixed] * MEMBERS + [pl.BlockSpec((model, cols), lambda s, info: (0, 0))],
            scratch_shapes=[
                pltpu.VMEM((heads, length, HD), BF),
                pltpu.VMEM((heads, length, HD), BF),
                pltpu.VMEM((heads, length, HD), F32),
                pltpu.VMEM((heads, length, HD), F32),
                pltpu.VMEM((MEMBERS, width, size), BF),
                pltpu.VMEM((MEMBERS, width, size), BF),
                pltpu.VMEM((cols, model), F32),
            ],
        ),
        out_shape=[jax.ShapeDtypeStruct((size, model), BF)] * MEMBERS
        + [jax.ShapeDtypeStruct((model, cols), BF)],
        compiler_params=params("arbitrary"),
        cost_estimate=pl.CostEstimate(
            flops=200 * heads * length * length * HD,
            transcendentals=heads * length * length // 2,
            bytes_accessed=20 * width * length,
        ),
        name="attention_backward",
    )(info, packed, *outs, *grads, logsum, normed, wt)


def hidden_body(groups, rows, info, tok, cot, m0, m1, m2, m3, vec_ref, down_ref, up_ref, out_w, *rest):
    (
        layer_out, resid_grad, a0, a1, a2, a3, stats, grads,
        low, unit, inverse, result, grad_n, act, grad_pre, stage, sems,
    ) = rest
    step = pl.program_id(0)
    member = info[1]
    vec = vec_ref[0:8, :].astype(F32)
    size, model = tok.shape
    width = model // MEMBERS
    units, piece = stage.shape[1], stage.shape[2]
    split, height, _ = grads.shape
    tall = height - (groups + 1) * (model // split)
    share = units // MEMBERS

    def out_rows(j):
        if split == 1:
            return out_w[0, pl.ds(pl.multiple_of((member ^ j) * width, width), width), :]
        unit_rows = out_w.shape[1]
        count = width // unit_rows
        return out_w[pl.ds((member ^ j) * count, count)].reshape(width, model)

    def drain(slot):
        pltpu.make_async_copy(stage.at[slot], stage.at[slot], sems.at[slot]).wait()

    def put(slot, block, down):
        for b in range(units):
            if split == 1:
                row, start = 0, block * model + b * piece
            elif down:
                per = tall // piece
                flat = block * units + b
                row, start = flat // per, (flat % per) * piece
            else:
                row, start = b, tall + (block - groups) * piece
            if not isinstance(start, int):
                start = pl.multiple_of(start, 16)
            pltpu.make_async_copy(
                stage.at[slot, b], grads.at[row, pl.ds(start, piece), :], sems.at[slot]
            ).start()

    @pl.when(step == 0)
    def _():
        branch = None
        for j, merged in enumerate((m0, m1, m2, m3)):
            part = contract(merged[...], out_rows(j), 0, 0)
            branch = part if branch is None else branch + part
        resid = tok[...].astype(F32) + vec[0:1] + branch
        normal, spread = normalize(resid)
        low[...] = (normal * vec[3:4] + vec[4:5]).astype(BF)
        unit[...] = normal
        inverse[...] = spread
        result[...] = resid
        grad_n[...] = jnp.zeros_like(grad_n)

    up = up_ref[...].reshape(model, model)
    down = down_ref[...].reshape(model, model)

    def tile(i, _):
        span = pl.ds(pl.multiple_of(i * rows, rows), rows)
        pre = contract(low[span, :], up, 1, 0)
        grad_act = contract(cot[span, :], down, 1, 1)
        square = pre * pre
        half = 0.5 + 0.5 * jnp.tanh(pre * (GELU_A + GELU_A * GELU_B * square))
        gelu = pre * half
        act_low = gelu.astype(BF)
        act[span, :] = act_low
        slope = half + gelu * (1.0 - half) * (2.0 * GELU_A + 6.0 * GELU_A * GELU_B * square)
        grad_low = (grad_act * slope).astype(BF)
        grad_pre[span, :] = grad_low
        result[span, :] += contract(act_low, down, 1, 0)
        grad_n[span, :] += contract(grad_low, up, 1, 1)
        return 0

    if rows == size:
        tile(0, 0)
    else:
        lax.fori_loop(0, size // rows, tile, 0)

    slot = 2 * (step % 2)

    @pl.when(step >= 2)
    def _():
        drain(slot)
        drain(slot + 1)

    stage[slot] = contract(act[...], cot[...], 0, 0).astype(BF).reshape(units, piece, model)
    put(slot, step, True)
    stage[slot + 1] = contract(low[...], grad_pre[...], 0, 0).astype(BF).reshape(units, piece, model)
    put(slot + 1, groups + step, False)

    @pl.when(step == groups - 1)
    def _():
        layer_out[...] = result[...].astype(BF)
        grad = grad_n[...]
        total = cot[...].astype(F32) + norm_backward(grad, vec[3:4], unit[...], inverse[...])
        resid_grad[...] = total
        branch = total.astype(BF)
        for j, out in enumerate((a0, a1, a2, a3)):
            out[...] = contract(out_rows(j), branch, 1, 1).astype(BF)
        stats[...] = jnp.zeros_like(stats)
        stats[0:1, :] = jnp.sum(grad * unit[...], axis=0, keepdims=True)
        stats[1:2, :] = jnp.sum(grad, axis=0, keepdims=True)
        other = 2 * (groups % 2)
        drain(other)
        for j, merged in enumerate((m0, m1, m2, m3)):
            block = contract(merged[...], branch, 1, 0).astype(BF)
            stage[other, pl.ds((member ^ j) * share, share)] = block.reshape(share, piece, model)
        put(other, 2 * groups, False)
        for which in range(4):
            drain(which)


def hidden_layer(info, tok, cot, merged, wt, weights, groups, rows=768):
    size, model = tok.shape
    width = model // MEMBERS
    split, height, _ = weights.shape
    unit = model // split
    tall = height - (groups + 1) * unit
    units = 8
    vec_block = wt.shape[0] // 64 - 1
    if split == 1:
        down_spec = pl.BlockSpec((1, model, model), lambda k, info: (0, k, 0))
        up_spec = pl.BlockSpec((1, model, model), lambda k, info: (0, groups + k, 0))
        out_spec = pl.BlockSpec(
            (1, model, model), lambda k, info: (0, 2 * groups, 0), pipeline_mode=pl.Buffered(1)
        )
    else:
        base = tall // unit
        down_spec = pl.BlockSpec((model // tall, tall, model), lambda k, info: (k, 0, 0))
        up_spec = pl.BlockSpec((split, unit, model), lambda k, info: (0, base + k, 0))
        out_spec = pl.BlockSpec(
            (split, unit, model),
            lambda k, info: (0, base + groups, 0),
            pipeline_mode=pl.Buffered(1),
        )

    def fixed(shape):
        zeros = (0,) * len(shape)
        return pl.BlockSpec(shape, lambda k, info: zeros)

    def shaped(shape, dtype):
        return jax.ShapeDtypeStruct(shape, dtype)

    return pl.pallas_call(
        functools.partial(hidden_body, groups, rows),
        grid_spec=pltpu.PrefetchScalarGridSpec(
            num_scalar_prefetch=1,
            grid=(groups,),
            in_specs=[whole((size, model))] * 2
            + [whole((width, size))] * MEMBERS
            + [
                pl.BlockSpec((64, model), lambda k, info: (vec_block, 0)),
                down_spec,
                up_spec,
                out_spec,
            ],
            out_specs=[fixed((size, model))] * 2
            + [fixed((width, size))] * MEMBERS
            + [fixed((8, model)), pl.BlockSpec(memory_space=pl.ANY)],
            scratch_shapes=[
                pltpu.VMEM((size, model), BF),
                pltpu.VMEM((size, model), F32),
                pltpu.VMEM((size, 1), F32),
                pltpu.VMEM((size, model), F32),
                pltpu.VMEM((size, model), F32),
                pltpu.VMEM((size, model), BF),
                pltpu.VMEM((size, model), BF),
                pltpu.VMEM((4, units, model // units, model), BF),
                pltpu.SemaphoreType.DMA((4,)),
            ],
        ),
        out_shape=[shaped((size, model), BF), shaped((size, model), F32)]
        + [shaped((width, size), BF)] * MEMBERS
        + [shaped((8, model), F32), shaped((split, height, model), BF)],
        compiler_params=params("arbitrary"),
        cost_estimate=pl.CostEstimate(
            flops=6 * size * model * (2 * groups + 1) * model,
            transcendentals=size * groups * model,
            bytes_accessed=4 * weights.size + 12 * size * model,
        ),
        name="hidden_layer",
    )(info, tok, cot, *merged, wt, weights, weights, weights)


def final_body(info, tok, p0, p1, p2, resid_grad, vec_ref, before, out, low, stats):
    step = pl.program_id(0)
    vec = vec_ref[0:8, :].astype(F32)
    unit, inverse = normalize(tok[...].astype(F32) + vec[0:1])
    grad = p0[...].astype(F32) + p1[...].astype(F32) + p2[...].astype(F32)
    result = resid_grad[...] + norm_backward(grad, vec[1:2], unit, inverse)
    out[...] = result
    low[...] = result.astype(BF)

    @pl.when(step == 0)
    def _():
        stats[...] = before[...]

    stats[2:3, :] += jnp.sum(grad * unit, axis=0, keepdims=True)
    stats[3:4, :] += jnp.sum(grad, axis=0, keepdims=True)
    stats[4:5, :] += jnp.sum(result, axis=0, keepdims=True)


def final_norm(info, tokens, parts, resid_grad, wt, before, rows=128):
    size, model = tokens.shape
    tok = pl.BlockSpec((rows, model), lambda s, info: (s, 0))
    one = pl.BlockSpec((8, model), lambda s, info: (0, 0))
    vec_block = wt.shape[0] // 64 - 1
    return pl.pallas_call(
        final_body,
        grid_spec=pltpu.PrefetchScalarGridSpec(
            num_scalar_prefetch=1,
            grid=(size // rows,),
            in_specs=[tok] * 5 + [pl.BlockSpec((64, model), lambda s, info: (vec_block, 0)), one],
            out_specs=[tok, tok, one],
        ),
        out_shape=[
            jax.ShapeDtypeStruct((size, model), F32),
            jax.ShapeDtypeStruct((size, model), BF),
            jax.ShapeDtypeStruct((8, model), F32),
        ],
        compiler_params=params("arbitrary"),
        cost_estimate=pl.CostEstimate(
            flops=30 * size * model, transcendentals=size, bytes_accessed=20 * size * model
        ),
        name="final_norm",
    )(info, tokens, *parts, resid_grad, wt, before)


def together(*values):
    return lax.optimization_barrier(values)


def on_device(
    groups_dp,
    inputs,
    pass_embed,
    gain_attend,
    shift_attend,
    attend_in,
    attend_out,
    gain_hidden,
    shift_hidden,
    hidden_up,
    hidden_down,
    cotangent,
):
    axes = ("dp", "seq")
    dp = groups_dp
    row = lax.axis_index("dp")
    line = lax.axis_index("seq")
    core = row & 1
    stays = core == (line >> 1)
    member = core * 2 + (line & 1)
    model = inputs.shape[2]
    width = model // MEMBERS
    share = attend_in.shape[0]
    groups = hidden_up.shape[1] // model

    def send(value, target):
        pairs = []
        for d in range(dp):
            for z in range(MEMBERS):
                goal = target(d, z)
                if goal is not None:
                    pairs.append((d * MEMBERS + z, goal[0] * MEMBERS + goal[1]))
        return lax.ppermute(value, axes, pairs)

    def at_home(d, z):
        return (d & 1) == (z >> 1)

    def swap(d, z):
        return None if at_home(d, z) else (d ^ 1, z ^ 2)

    def other_core(d, z):
        return (d ^ 1, z)

    def next_chip(d, z):
        return (d, z ^ 1)

    mine = inputs[0]
    first = send(mine, lambda d, z: (d, z ^ 1) if at_home(d, z) else (d ^ 1, z ^ 2))
    mine_other = send(mine, other_core)

    columns = attend_in.reshape(share, 3, MEMBERS, width).transpose(2, 0, 1, 3)
    columns = columns.reshape(MEMBERS, share, 3 * width)
    vectors = jnp.stack([pass_embed, gain_attend, shift_attend, gain_hidden, shift_hidden], axis=1)
    vectors = jnp.pad(vectors, ((0, 0), (0, 59)))

    def for_member(which):
        piece = lax.dynamic_index_in_dim(columns, which, 0, keepdims=False)
        return jnp.concatenate([piece, vectors], axis=1)

    def ordered(which, low_piece, high_piece):
        return jnp.where(
            which,
            jnp.concatenate([high_piece, low_piece]),
            jnp.concatenate([low_piece, high_piece]),
        )

    def is_upper(bit):
        return ((row >> bit) & 1) == 1

    def flipped(mask):
        return lambda d, z: (d ^ mask, z)

    bits = dp.bit_length() - 1
    own = for_member(member)[None]
    gathered = ordered(is_upper(0), own, send(for_member(member ^ 2), other_core)[None])
    bit = 1
    while bit < bits:
        near = ordered(is_upper(bit), gathered, send(gathered, flipped(1 << bit)))
        if bit + 1 < bits:
            far = ordered(
                is_upper(bit),
                send(gathered, flipped(2 << bit)),
                send(gathered, flipped(3 << bit)),
            )
            near = ordered(is_upper(bit + 1), near, far)
        gathered = near
        bit += 2
    first, gathered = together(first, gathered)
    wt = gathered.reshape(model, 3 * width + 64).T
    late = send(first, lambda d, z: None if at_home(d, z) else (d, z ^ 1))
    first_other = send(first, other_core)

    pack = jnp.concatenate(
        [hidden_down]
        + [hidden_up[:, k * model : (k + 1) * model] for k in range(groups)]
        + [attend_out]
    )
    height = pack.shape[0]
    weights = lax.all_gather(pack, "dp", axis=0, tiled=False)
    split = dp if (model // dp) % 96 == 0 else 1
    if split == 1:
        tall = hidden_down.shape[0]
        down = weights[:, :tall].reshape(1, dp * tall, model)
        others = weights[:, tall:].reshape(dp, groups + 1, share, model).transpose(1, 0, 2, 3)
        weights = jnp.concatenate([down, others.reshape(1, -1, model)], axis=1)

    stay_flag = stays.astype(jnp.int32)
    early = jnp.where(stays, member, member ^ 2)
    info = jnp.stack([stay_flag, member, core]).astype(jnp.int32)
    info_early = jnp.stack([stay_flag, early, early ^ 1]).astype(jnp.int32)
    info_late = jnp.stack([stay_flag, early ^ 2, early ^ 3]).astype(jnp.int32)
    carried = project(info_early, mine, mine_other, first, first_other, wt, None)
    late, packed = together(late, carried[0])
    late_other = send(late, other_core)
    packed, normed = project(
        info_late, first_other, first, late_other, late, wt, [packed, carried[1]]
    )
    grad_mine, packed = together(cotangent[0], packed)
    grad_moved = send(grad_mine, swap)

    *outs, logsum = attend_forward(info, packed)
    mine, first, logsum = together(mine, first, logsum)
    routes = [None, next_chip, other_core, lambda d, z: (d ^ 1, z ^ 1)]
    merged = [outs[0]] + [send(outs[j], routes[j]) for j in (1, 3, 2)]
    merged = [merged[0], merged[1], merged[3], merged[2]]

    tokens = jnp.where(stays, mine, first)
    cot = jnp.where(stays, grad_mine, grad_moved)
    layer_out, resid_grad, a0, a1, a2, a3, stats, grads = hidden_layer(
        info, tokens, cot, merged, wt, weights, groups
    )
    r1 = send(a1, routes[1])
    r3 = send(a3, routes[3])
    r2 = send(a2, routes[2])
    if split == 1:
        tall = hidden_down.shape[0]
        down = grads[0, : dp * tall].reshape(dp, tall, model)
        others = grads[0, dp * tall :].reshape(groups + 1, dp, share, model).transpose(1, 0, 2, 3)
        grads = jnp.concatenate([down, others.reshape(dp, -1, model)], axis=1)
    reduced = lax.psum_scatter(grads, "dp", scatter_dimension=0, tiled=True)[0]
    layer_out, r3 = together(layer_out, r3)
    layer_moved = send(layer_out, swap)
    n0, n1, n2, n3, dw = attend_backward(
        info, packed, outs, [a0, r1, r2, r3], logsum, normed, wt
    )
    n3, n2, layer_moved = together(n3, n2, layer_moved)
    c3 = send(n3, other_core)
    c2 = send(n2, other_core)
    partial = (n1.astype(F32) + c3.astype(F32)).astype(BF)
    partial, dw, reduced = together(partial, dw, reduced)
    scattered = lax.psum_scatter(reduced, "seq", scatter_dimension=0, tiled=True)
    z1 = send(partial, next_chip)
    z1, scattered = together(z1, scattered)
    total = lax.all_gather(scattered, "seq", axis=0, tiled=True)
    input_grad, input_low, stats = final_norm(
        info, tokens, [n0, c2, z1], resid_grad, wt, stats
    )
    input_moved = send(input_low, swap)

    current = dw.reshape(dp, share, 3 * width)
    top = bits - 1
    while top > 0:
        width_bits = 2 if top > 1 else 1
        quarter = current.shape[0] >> width_bits
        low_bit = top - width_bits + 1
        mine_at = (row >> low_bit) & ((1 << width_bits) - 1)

        def piece(j):
            return lax.dynamic_slice_in_dim(current, (mine_at ^ j) * quarter, quarter, 0)

        summed = piece(0).astype(F32)
        for j in range(1, 1 << width_bits):
            summed = summed + send(piece(j), flipped(j << low_bit)).astype(F32)
        current = summed.astype(BF)
        top -= width_bits
    got = send(current, lambda d, z: (d, z ^ 2))
    current = (current.astype(F32) + got.astype(F32)).astype(BF)
    upper = core == 1
    give = jnp.where(upper, current[0], current[1])
    keep = jnp.where(upper, current[1], current[0])
    got = send(give, other_core)
    pair = jnp.where(upper, jnp.stack([got, keep]), jnp.stack([keep, got]))
    far = send(pair, next_chip)
    odd = (line & 1) == 1
    quad = [
        jnp.where(odd, far[0], pair[0]),
        jnp.where(odd, pair[0], far[0]),
        jnp.where(odd, far[1], pair[1]),
        jnp.where(odd, pair[1], far[1]),
    ]
    proj_grad = jnp.concatenate(
        [q[:, p * width : (p + 1) * width] for p in range(3) for q in quad], axis=1
    ).astype(F32)

    stats = stats + send(stats, other_core)
    stats, total = together(stats, total)
    total = total.astype(F32)
    flips = []
    bit = 1
    while bit < bits:
        wide = 2 if bit + 1 < bits else 1
        flips.append([flipped(j << bit) for j in range(1, 1 << wide)])
        bit += wide
    flips.append([lambda d, z, j=j: (d, z ^ j) for j in range(1, MEMBERS)])
    for targets in flips:
        stats = sum([send(stats, t) for t in targets], stats)
    small = lax.dynamic_slice(stats, (0, row * share), (8, share))

    tall = hidden_down.shape[0]
    down_grad = total[:tall]
    up_grad = jnp.concatenate(
        [total[tall + k * share : tall + (k + 1) * share] for k in range(groups)], axis=1
    )
    out_grad = total[tall + groups * share :]
    return (
        jnp.where(stays, layer_out, layer_moved)[None],
        jnp.where(stays, input_grad, input_moved.astype(F32))[None],
        small[4],
        small[2],
        small[3],
        proj_grad,
        out_grad,
        small[0],
        small[1],
        up_grad,
        down_grad,
    )


def solution(mesh):
    vector, matrix, tokens = P("dp"), P("dp", None), P("dp", "seq", None)
    return jax.shard_map(
        functools.partial(on_device, mesh.shape["dp"]),
        mesh=mesh,
        in_specs=(
            tokens,
            vector,
            vector,
            vector,
            matrix,
            matrix,
            vector,
            vector,
            matrix,
            matrix,
            tokens,
        ),
        out_specs=(
            tokens,
            tokens,
            vector,
            vector,
            vector,
            matrix,
            matrix,
            vector,
            vector,
            matrix,
            matrix,
        ),
        check_vma=False,
    )
```

```python
import functools

import jax
import jax.numpy as jnp
from jax import lax
from jax.experimental import pallas as pl
from jax.experimental.pallas import tpu as pltpu
from jax.sharding import PartitionSpec as P

HD = 64
EPSILON = 1e-05
MASKED = -1e30
F32 = jnp.float32
BF = jnp.bfloat16
MEMBERS = 4
VMEM_LIMIT = 60 << 20
GELU_A = 0.7978845608028654
GELU_B = 0.044715


def contract(left, right, left_dim, right_dim):
    return lax.dot_general(
        left, right, (((left_dim,), (right_dim,)), ((), ())), preferred_element_type=F32
    )


def normalize(hidden):
    center = hidden - jnp.mean(hidden, axis=-1, keepdims=True)
    spread = jnp.mean(center * center, axis=-1, keepdims=True)
    inverse = lax.rsqrt(spread + EPSILON)
    return center * inverse, inverse


def norm_backward(grad, gain, unit, inverse):
    scaled = grad * gain
    return inverse * (
        scaled
        - jnp.mean(scaled, axis=-1, keepdims=True)
        - unit * jnp.mean(scaled * unit, axis=-1, keepdims=True)
    )


def params(*semantics):
    return pltpu.CompilerParams(dimension_semantics=semantics, vmem_limit_bytes=VMEM_LIMIT)


def whole(shape):
    zeros = (0,) * len(shape)
    return pl.BlockSpec(shape, lambda *_: zeros, pipeline_mode=pl.Buffered(1))


def project_body(count, info, *refs):
    sources, wt = refs[: 2 * count], refs[2 * count]
    packed, normed = refs[-2:]
    slot = pl.program_id(0)
    stay = info[0] > 0
    cols = wt.shape[0] - 64
    vec = wt[cols : cols + 8, :].astype(F32)
    for which in range(count):
        for wanted in (True, False):
            source = sources[2 * which + (0 if wanted else 1)]

            @pl.when(jnp.logical_and(slot == which, stay == wanted))
            def _(source=source):
                unit, _ = normalize(source[...].astype(F32) + vec[0:1])
                normed[...] = (unit * vec[1:2] + vec[2:3]).astype(BF)

    packed[...] = contract(wt[:cols, :], normed[...], 1, 1).astype(BF)


def project(info, sources, wt, carried, rows=384):
    chunk, width = sources[0].shape
    count = len(sources) // 2
    cols = wt.shape[0] - 64
    length = MEMBERS * chunk
    per = chunk // rows

    def src(which, wanted):
        def index(s, b, info):
            block = jnp.where(s == which, b, (per - 1) * (s > which))
            return (jnp.where(info[0] == wanted, block, 0), 0)

        return pl.BlockSpec((rows, width), index)

    def place(s, b, info):
        return info[1 + s] * per + b

    in_specs = [src(w, f) for w in range(count) for f in (1, 0)] + [whole(wt.shape)]
    aliases = {}
    args = [info, *sources, wt]
    if carried is not None:
        in_specs += [pl.BlockSpec(memory_space=pl.ANY)] * 2
        aliases = {2 * count + 2: 0, 2 * count + 3: 1}
        args += list(carried)
    return pl.pallas_call(
        functools.partial(project_body, count),
        grid_spec=pltpu.PrefetchScalarGridSpec(
            num_scalar_prefetch=1,
            grid=(count, per),
            in_specs=in_specs,
            out_specs=[
                pl.BlockSpec((cols, rows), lambda s, b, info: (0, place(s, b, info))),
                pl.BlockSpec((rows, width), lambda s, b, info: (place(s, b, info), 0)),
            ],
        ),
        out_shape=[
            jax.ShapeDtypeStruct((cols, length), BF),
            jax.ShapeDtypeStruct((length, width), BF),
        ],
        input_output_aliases=aliases,
        compiler_params=params("arbitrary", "arbitrary"),
        cost_estimate=pl.CostEstimate(
            flops=2 * count * chunk * width * cols,
            transcendentals=count * chunk,
            bytes_accessed=6 * count * chunk * width,
        ),
        name="norm_project",
    )(*args)


def diagonal(size):
    key = lax.broadcasted_iota(jnp.int32, (size, size), 0)
    query = lax.broadcasted_iota(jnp.int32, (size, size), 1)
    return key <= query


def forward_body(heads, info, packed, out0, out1, out2, out3, logsum, keys):
    step = pl.program_id(0)
    width = heads * HD
    size = out0.shape[1]
    scale = BF(HD**-0.5)

    @pl.when(step == 0)
    def _():
        for h in range(heads):
            keys[h] = packed[width + h * HD : width + (h + 1) * HD, :].T

    first = pl.multiple_of(step * size, size)
    queries = [packed[h * HD : (h + 1) * HD, pl.ds(first, size)] * scale for h in range(heads)]

    def block(span, carry, allowed, part):
        all_scores = [
            contract(keys[h, span, :], queries[h][:, part], 1, 0) for h in range(heads)
        ]
        result = []
        for h in range(heads):
            top, total, summed = carry[h]
            scores = all_scores[h]
            if allowed is not None:
                scores = jnp.where(allowed, scores, MASKED)
            new_top = jnp.maximum(top, jnp.max(scores, axis=0, keepdims=True))
            weights = jnp.exp(scores - new_top)
            shrink = jnp.exp(top - new_top)
            total = total * shrink + jnp.sum(weights, axis=0, keepdims=True)
            values = packed[2 * width + h * HD : 2 * width + (h + 1) * HD, span]
            summed = summed * shrink + contract(values, weights.astype(BF), 1, 0)
            result.append((new_top, total, summed))
        return tuple(result)

    begin = tuple(
        (
            jnp.full((1, size), MASKED, F32),
            jnp.zeros((1, size), F32),
            jnp.zeros((HD, size), F32),
        )
        for _ in range(heads)
    )
    carry = lax.fori_loop(
        0,
        step,
        lambda j, c: block(pl.ds(pl.multiple_of(j * size, size), size), c, None, slice(0, size)),
        begin,
    )
    half = size // 2
    lower, upper = pl.ds(first, half), pl.ds(pl.multiple_of(first + half, half), half)
    allowed = diagonal(half)
    left = [tuple(v[:, :half] for v in c) for c in carry]
    right = [tuple(v[:, half:] for v in c) for c in carry]
    left = block(lower, left, allowed, slice(0, half))
    right = block(lower, right, None, slice(half, size))
    right = block(upper, right, allowed, slice(half, size))
    carry = [
        tuple(jnp.concatenate([a, b], axis=1) for a, b in zip(l, r)) for l, r in zip(left, right)
    ]
    place = step ^ info[1]
    for h in range(heads):
        top, total, summed = carry[h]
        logsum[h : h + 1, :] = top + jnp.log(total)
        low = (summed / total).astype(BF)
        for j, out in enumerate((out0, out1, out2, out3)):

            @pl.when(place == j)
            def _(out=out, low=low, h=h):
                out[h * HD : (h + 1) * HD, :] = low


def attend_forward(info, packed):
    cols, length = packed.shape
    heads = cols // (3 * HD)
    width = heads * HD
    size = length // MEMBERS
    part = jax.ShapeDtypeStruct((width, size), BF)
    return pl.pallas_call(
        functools.partial(forward_body, heads),
        grid_spec=pltpu.PrefetchScalarGridSpec(
            num_scalar_prefetch=1,
            grid=(MEMBERS,),
            in_specs=[whole(packed.shape)],
            out_specs=[pl.BlockSpec((width, size), lambda s, info: (0, 0))] * MEMBERS
            + [pl.BlockSpec((8, size), lambda s, info: (0, s))],
            scratch_shapes=[pltpu.VMEM((heads, length, HD), BF)],
        ),
        out_shape=[part] * MEMBERS + [jax.ShapeDtypeStruct((8, length), F32)],
        compiler_params=params("arbitrary"),
        cost_estimate=pl.CostEstimate(
            flops=heads * length * HD, transcendentals=length, bytes_accessed=width * length
        ),
        name="attention_forward",
    )(info, packed)


def backward_body(heads, top, info, packed, o0, o1, o2, o3, g0, g1, g2, g3, logsum, wt, *rest):
    last_stage = top == 1
    keys, values, grad_keys, grad_values, out_all, grad_all = rest[-6:]
    if last_stage:
        keys_in, values_in, near, far, stacked_out = rest[:-6]
    else:
        near, far, stacked_out, keys_out, values_out = rest[:-6]
    step = pl.program_id(0)
    chunk_id = top - step
    width = heads * HD
    size = near.shape[0]
    scale = BF(HD**-0.5)

    @pl.when(step == 0)
    def _():
        for h in range(heads):
            keys[h] = packed[width + h * HD : width + (h + 1) * HD, :].T
            values[h] = packed[2 * width + h * HD : 2 * width + (h + 1) * HD, :].T
        if last_stage:
            grad_keys[...] = keys_in[...]
            grad_values[...] = values_in[...]
        else:
            grad_keys[...] = jnp.zeros_like(grad_keys)
            grad_values[...] = jnp.zeros_like(grad_values)
        for j, (o, g) in enumerate(((o0, g0), (o1, g1), (o2, g2), (o3, g3))):
            out_all[info[1] ^ j] = o[...]
            grad_all[info[1] ^ j] = g[...]

    first = pl.multiple_of(chunk_id * size, size)
    rows = [slice(h * HD, (h + 1) * HD) for h in range(heads)]
    query_t = [packed[r, pl.ds(first, size)] * scale for r in rows]
    query = [q.T for q in query_t]
    grad_t = [grad_all[chunk_id, r, :] for r in rows]
    grad = [g.T for g in grad_t]
    delta = [
        jnp.sum(g.astype(F32) * out_all[chunk_id, r, :].astype(F32), axis=0, keepdims=True)
        for g, r in zip(grad_t, rows)
    ]
    lse = [logsum[h : h + 1, :] for h in range(heads)]

    def block(span, carry, allowed, part):
        result = []
        for h in range(heads):
            scores = contract(keys[h, span, :], query_t[h][:, part], 1, 0)
            grad_probs = contract(values[h, span, :], grad_t[h][:, part], 1, 0)
            probs = jnp.exp(scores - lse[h][:, part])
            if allowed is not None:
                probs = jnp.where(allowed, probs, 0.0)
            grad_scores = (probs * (grad_probs - delta[h][:, part])).astype(BF)
            grad_values[h, span, :] += contract(probs.astype(BF), grad[h][part], 1, 0)
            grad_keys[h, span, :] += contract(grad_scores, query[h][part], 1, 0)
            keys_t = packed[width + h * HD : width + (h + 1) * HD, span]
            result.append(carry[h] + contract(keys_t, grad_scores, 1, 0))
        return tuple(result)

    grad_query = tuple(jnp.zeros((HD, size), F32) for _ in range(heads))
    grad_query = lax.fori_loop(
        0,
        chunk_id,
        lambda j, c: block(pl.ds(pl.multiple_of(j * size, size), size), c, None, slice(0, size)),
        grad_query,
    )
    half = size // 2
    lower, upper = pl.ds(first, half), pl.ds(pl.multiple_of(first + half, half), half)
    allowed = diagonal(half)
    left = block(lower, [g[:, :half] for g in grad_query], allowed, slice(0, half))
    right = block(lower, [g[:, half:] for g in grad_query], None, slice(half, size))
    right = block(upper, right, allowed, slice(half, size))
    grad_query = [jnp.concatenate([a, b], axis=1) for a, b in zip(left, right)]
    pieces = [(g * HD**-0.5).astype(BF) for g in grad_query]
    pieces += [grad_keys[h, pl.ds(first, size), :].astype(BF).T for h in range(heads)]
    pieces += [grad_values[h, pl.ds(first, size), :].astype(BF).T for h in range(heads)]
    stacked = jnp.concatenate(pieces, axis=0)
    partial = contract(stacked, wt[: 3 * width, :], 0, 0).astype(BF)
    is_near = ((chunk_id ^ info[1]) & 1) == 0

    @pl.when(is_near)
    def _():
        near[...] = partial

    @pl.when(jnp.logical_not(is_near))
    def _():
        far[...] = partial

    stacked_out[...] = stacked
    if not last_stage:

        @pl.when(step == 1)
        def _():
            left = keys_out.shape[1]
            keys_out[...] = grad_keys[:, :left, :]
            values_out[...] = grad_values[:, :left, :]


def attend_backward(info, packed, outs, grads, logsum, wt, carried=None):
    cols, length = packed.shape
    heads = cols // (3 * HD)
    width = heads * HD
    size = length // MEMBERS
    model = wt.shape[1]
    top = MEMBERS - 1 if carried is None else 1
    span = (top + 1) * size
    left = length // 2

    def fixed(shape):
        zeros = (0,) * len(shape)
        return pl.BlockSpec(shape, lambda s, info: zeros)

    partial = jax.ShapeDtypeStruct((size, model), BF)
    state = jax.ShapeDtypeStruct((heads, left, HD), F32)
    in_specs = (
        [whole((cols, span))]
        + [whole((width, size))] * (2 * MEMBERS)
        + [
            pl.BlockSpec((8, size), lambda s, info: (0, top - s)),
            whole(wt.shape),
        ]
    )
    out_shape = [partial, partial, jax.ShapeDtypeStruct((cols, 2 * size), BF)]
    out_specs = [fixed((size, model))] * 2
    out_specs += [pl.BlockSpec((cols, size), lambda s, info: (0, 1 - s))]
    if carried is None:
        more = ()
        out_shape += [state, state]
        out_specs += [fixed(state.shape)] * 2
    else:
        more = tuple(carried)
        in_specs += [whole(state.shape)] * 2
    blocks = 7 if carried is None else 3
    return pl.pallas_call(
        functools.partial(backward_body, heads, top),
        grid_spec=pltpu.PrefetchScalarGridSpec(
            num_scalar_prefetch=1,
            grid=(2,),
            in_specs=in_specs,
            out_specs=out_specs,
            scratch_shapes=[
                pltpu.VMEM((heads, span, HD), BF),
                pltpu.VMEM((heads, span, HD), BF),
                pltpu.VMEM((heads, span, HD), F32),
                pltpu.VMEM((heads, span, HD), F32),
                pltpu.VMEM((MEMBERS, width, size), BF),
                pltpu.VMEM((MEMBERS, width, size), BF),
            ],
        ),
        out_shape=out_shape,
        compiler_params=params("arbitrary"),
        cost_estimate=pl.CostEstimate(
            flops=200 * heads * blocks * size * size * HD,
            transcendentals=heads * blocks * size * size,
            bytes_accessed=20 * width * length,
        ),
        name="attention_backward",
    )(info, packed, *outs, *grads, logsum, wt, *more)


def project_grad_body(*refs):
    stacked, normed = refs[:2]
    out, total = refs[-2:]
    step = pl.program_id(0)
    part = contract(stacked[...], normed[...], 1, 0)

    @pl.when(step == 0)
    def _():
        total[...] = part if len(refs) == 4 else refs[2][...] + part

    @pl.when(step == 1)
    def _():
        if len(refs) == 4:
            out[...] = total[...] + part
        else:
            out[...] = (total[...] + part).astype(BF).T


def project_grad(stacked, normed, half, before=None):
    cols, span = stacked.shape
    size = span // 2
    model = normed.shape[1]
    more = () if before is None else (before,)
    if before is None:
        out = jax.ShapeDtypeStruct((cols, model), F32)
    else:
        out = jax.ShapeDtypeStruct((model, cols), BF)
    return pl.pallas_call(
        project_grad_body,
        grid=(2,),
        in_specs=[
            pl.BlockSpec((cols, size), lambda s: (0, s)),
            pl.BlockSpec((size, model), lambda s: (2 * half + s, 0)),
        ]
        + [whole((cols, model))] * len(more),
        out_specs=pl.BlockSpec(out.shape, lambda s: (0, 0)),
        out_shape=out,
        scratch_shapes=[pltpu.VMEM((cols, model), F32)],
        compiler_params=params("arbitrary"),
        cost_estimate=pl.CostEstimate(
            flops=2 * cols * span * model, transcendentals=0, bytes_accessed=2 * span * (cols + model)
        ),
        name="project_grad",
    )(stacked, normed, *more)


def hidden_body(groups, rows, info, tok, cot, m0, m1, m2, m3, vec_ref, down_ref, up_ref, out_w, *rest):
    (
        layer_out, resid_grad, a0, a1, a2, a3, stats, down_own, down_other, grads,
        low, unit, inverse, result, grad_n, act, grad_pre, stage, sems,
    ) = rest
    step = pl.program_id(0)
    member = info[1]
    vec = vec_ref[0:8, :].astype(F32)
    size, model = tok.shape
    width = model // MEMBERS
    units, piece = stage.shape[1], stage.shape[2]
    split = grads.shape[0]
    share = units // MEMBERS

    def out_rows(j):
        if split == 1:
            return out_w[0, pl.ds(pl.multiple_of((member ^ j) * width, width), width), :]
        unit_rows = out_w.shape[1]
        count = width // unit_rows
        return out_w[pl.ds((member ^ j) * count, count)].reshape(width, model)

    def drain(slot):
        pltpu.make_async_copy(stage.at[slot], stage.at[slot], sems.at[slot]).wait()

    def put_down(slot, block):
        for b in range(units):
            source = stage.at[slot, b]
            if split == 1:
                start = pl.multiple_of(block * model + b * piece, 16)
                target = down_own.at[0, pl.ds(start, piece), :]
                pltpu.make_async_copy(source, target, sems.at[slot]).start()
                continue
            per = units // 2
            rows_at = slice((b % per) * piece, (b % per + 1) * piece)
            for wanted, array in ((True, down_own), (False, down_other)):

                @pl.when((info[2] == b // per) == wanted)
                def _(array=array, source=source, rows_at=rows_at):
                    target = array.at[block, rows_at, :]
                    pltpu.make_async_copy(source, target, sems.at[slot]).start()

    def put(slot, block):
        for b in range(units):
            if split == 1:
                row, start = 0, block * model + b * piece
            else:
                row, start = b, block * piece
            if not isinstance(start, int):
                start = pl.multiple_of(start, 16)
            pltpu.make_async_copy(
                stage.at[slot, b], grads.at[row, pl.ds(start, piece), :], sems.at[slot]
            ).start()

    @pl.when(step == 0)
    def _():
        branch = None
        for j, merged in enumerate((m0, m1, m2, m3)):
            part = contract(merged[...], out_rows(j), 0, 0)
            branch = part if branch is None else branch + part
        resid = tok[...].astype(F32) + vec[0:1] + branch
        normal, spread = normalize(resid)
        low[...] = (normal * vec[3:4] + vec[4:5]).astype(BF)
        unit[...] = normal
        inverse[...] = spread
        result[...] = resid
        grad_n[...] = jnp.zeros_like(grad_n)

    up = up_ref[...].reshape(model, model)
    down = down_ref[...].reshape(model, model)

    def tile(i, _):
        span = pl.ds(pl.multiple_of(i * rows, rows), rows)
        pre = contract(low[span, :], up, 1, 0)
        grad_act = contract(cot[span, :], down, 1, 1)
        square = pre * pre
        half = 0.5 + 0.5 * jnp.tanh(pre * (GELU_A + GELU_A * GELU_B * square))
        gelu = pre * half
        act_low = gelu.astype(BF)
        act[span, :] = act_low
        slope = half + gelu * (1.0 - half) * (2.0 * GELU_A + 6.0 * GELU_A * GELU_B * square)
        grad_low = (grad_act * slope).astype(BF)
        grad_pre[span, :] = grad_low
        result[span, :] += contract(act_low, down, 1, 0)
        grad_n[span, :] += contract(grad_low, up, 1, 1)
        return 0

    if rows == size:
        tile(0, 0)
    else:
        lax.fori_loop(0, size // rows, tile, 0)

    slot = 2 * (step % 2)

    @pl.when(step >= 2)
    def _():
        drain(slot)
        drain(slot + 1)

    stage[slot] = contract(act[...], cot[...], 0, 0).astype(BF).reshape(units, piece, model)
    put_down(slot, step)
    stage[slot + 1] = contract(low[...], grad_pre[...], 0, 0).astype(BF).reshape(units, piece, model)
    put(slot + 1, step)

    @pl.when(step == groups - 1)
    def _():
        layer_out[...] = result[...].astype(BF)
        grad = grad_n[...]
        total = cot[...].astype(F32) + norm_backward(grad, vec[3:4], unit[...], inverse[...])
        resid_grad[...] = total
        branch = total.astype(BF)
        for j, out in enumerate((a0, a1, a2, a3)):
            out[...] = contract(out_rows(j), branch, 1, 1).astype(BF)
        stats[...] = jnp.zeros_like(stats)
        stats[0:1, :] = jnp.sum(grad * unit[...], axis=0, keepdims=True)
        stats[1:2, :] = jnp.sum(grad, axis=0, keepdims=True)
        other = 2 * (groups % 2)
        drain(other)
        for j, merged in enumerate((m0, m1, m2, m3)):
            block = contract(merged[...], branch, 1, 0).astype(BF)
            stage[other, pl.ds((member ^ j) * share, share)] = block.reshape(share, piece, model)
        put(other, groups)
        for which in range(4):
            drain(which)


def hidden_layer(info, tok, cot, merged, wt, weights, groups, rows=768):
    size, model = tok.shape
    width = model // MEMBERS
    split, height, _ = weights.shape
    unit = model // split
    tall = height - (groups + 1) * unit
    units = 8
    vec_block = wt.shape[0] // 64 - 1
    down_shape = (1, tall, model) if split == 1 else (split // 2, tall, model)
    if split == 1:
        down_spec = pl.BlockSpec((1, model, model), lambda k, info: (0, k, 0))
        up_spec = pl.BlockSpec((1, model, model), lambda k, info: (0, groups + k, 0))
        out_spec = pl.BlockSpec(
            (1, model, model), lambda k, info: (0, 2 * groups, 0), pipeline_mode=pl.Buffered(1)
        )
    else:
        base = tall // unit
        down_spec = pl.BlockSpec((model // tall, tall, model), lambda k, info: (k, 0, 0))
        up_spec = pl.BlockSpec((split, unit, model), lambda k, info: (0, base + k, 0))
        out_spec = pl.BlockSpec(
            (split, unit, model),
            lambda k, info: (0, base + groups, 0),
            pipeline_mode=pl.Buffered(1),
        )

    def fixed(shape):
        zeros = (0,) * len(shape)
        return pl.BlockSpec(shape, lambda k, info: zeros)

    def shaped(shape, dtype):
        return jax.ShapeDtypeStruct(shape, dtype)

    return pl.pallas_call(
        functools.partial(hidden_body, groups, rows),
        grid_spec=pltpu.PrefetchScalarGridSpec(
            num_scalar_prefetch=1,
            grid=(groups,),
            in_specs=[whole((size, model))] * 2
            + [whole((width, size))] * MEMBERS
            + [
                pl.BlockSpec((64, model), lambda k, info: (vec_block, 0)),
                down_spec,
                up_spec,
                out_spec,
            ],
            out_specs=[fixed((size, model))] * 2
            + [fixed((width, size))] * MEMBERS
            + [fixed((8, model))]
            + [pl.BlockSpec(memory_space=pl.ANY)] * 3,
            scratch_shapes=[
                pltpu.VMEM((size, model), BF),
                pltpu.VMEM((size, model), F32),
                pltpu.VMEM((size, 1), F32),
                pltpu.VMEM((size, model), F32),
                pltpu.VMEM((size, model), F32),
                pltpu.VMEM((size, model), BF),
                pltpu.VMEM((size, model), BF),
                pltpu.VMEM((4, units, model // units, model), BF),
                pltpu.SemaphoreType.DMA((4,)),
            ],
        ),
        out_shape=[shaped((size, model), BF), shaped((size, model), F32)]
        + [shaped((width, size), BF)] * MEMBERS
        + [
            shaped((8, model), F32),
            shaped(down_shape, BF),
            shaped(down_shape if split > 1 else (1, 16, model), BF),
            shaped((split, (groups + 1) * unit, model), BF),
        ],
        compiler_params=params("arbitrary"),
        cost_estimate=pl.CostEstimate(
            flops=6 * size * model * (2 * groups + 1) * model,
            transcendentals=size * groups * model,
            bytes_accessed=4 * weights.size + 12 * size * model,
        ),
        name="hidden_layer",
    )(info, tok, cot, *merged, wt, weights, weights, weights)


def final_body(owner, info, tok, p0, p1, p2, resid_grad, vec_ref, before, *rest):
    out, low, stats = rest[-3:]
    step = pl.program_id(0)
    mine = info[2] == owner
    vec = vec_ref[0:8, :].astype(F32)

    @pl.when(step == 0)
    def _():
        stats[...] = before[...]

    @pl.when(mine)
    def _():
        unit, inverse = normalize(tok[...].astype(F32) + vec[0:1])
        grad = p0[...].astype(F32) + p1[...].astype(F32) + p2[...].astype(F32)
        result = resid_grad[...] + norm_backward(grad, vec[1:2], unit, inverse)
        out[...] = result
        low[...] = result.astype(BF)
        stats[2:3, :] += jnp.sum(grad * unit, axis=0, keepdims=True)
        stats[3:4, :] += jnp.sum(grad, axis=0, keepdims=True)
        stats[4:5, :] += jnp.sum(result, axis=0, keepdims=True)

    if len(rest) == 4:

        @pl.when(jnp.logical_not(mine))
        def _():
            out[...] = rest[0][...]


def final_norm(owner, info, tokens, parts, resid_grad, wt, before, earlier=None, rows=384):
    size, model = tokens.shape
    tok = pl.BlockSpec((rows, model), lambda s, info: (s, 0))
    one = pl.BlockSpec((8, model), lambda s, info: (0, 0))
    vec_block = wt.shape[0] // 64 - 1
    more = () if earlier is None else (earlier,)
    return pl.pallas_call(
        functools.partial(final_body, owner),
        grid_spec=pltpu.PrefetchScalarGridSpec(
            num_scalar_prefetch=1,
            grid=(size // rows,),
            in_specs=[tok] * 5
            + [pl.BlockSpec((64, model), lambda s, info: (vec_block, 0)), one]
            + [tok] * len(more),
            out_specs=[tok, tok, one],
        ),
        out_shape=[
            jax.ShapeDtypeStruct((size, model), F32),
            jax.ShapeDtypeStruct((size, model), BF),
            jax.ShapeDtypeStruct((8, model), F32),
        ],
        compiler_params=params("arbitrary"),
        cost_estimate=pl.CostEstimate(
            flops=size * model, transcendentals=size, bytes_accessed=size * model
        ),
        name="final_norm",
    )(info, tokens, *parts, resid_grad, wt, before, *more)


def together(*values):
    return lax.optimization_barrier(values)


def on_device(
    groups_dp,
    inputs,
    pass_embed,
    gain_attend,
    shift_attend,
    attend_in,
    attend_out,
    gain_hidden,
    shift_hidden,
    hidden_up,
    hidden_down,
    cotangent,
):
    axes = ("dp", "seq")
    dp = groups_dp
    row = lax.axis_index("dp")
    line = lax.axis_index("seq")
    core = row & 1
    stays = core == (line >> 1)
    member = core * 2 + (line & 1)
    model = inputs.shape[2]
    width = model // MEMBERS
    share = attend_in.shape[0]
    groups = hidden_up.shape[1] // model

    def send(value, target):
        pairs = []
        for d in range(dp):
            for z in range(MEMBERS):
                goal = target(d, z)
                if goal is not None:
                    pairs.append((d * MEMBERS + z, goal[0] * MEMBERS + goal[1]))
        return lax.ppermute(value, axes, pairs)

    def at_home(d, z):
        return (d & 1) == (z >> 1)

    def swap(d, z):
        return None if at_home(d, z) else (d ^ 1, z ^ 2)

    def other_core(d, z):
        return (d ^ 1, z)

    def next_chip(d, z):
        return (d, z ^ 1)

    mine = inputs[0]
    first = send(mine, lambda d, z: (d, z ^ 1) if at_home(d, z) else (d ^ 1, z ^ 2))
    mine_other = send(mine, other_core)

    columns = attend_in.reshape(share, 3, MEMBERS, width).transpose(2, 0, 1, 3)
    columns = columns.reshape(MEMBERS, share, 3 * width)
    vectors = jnp.stack([pass_embed, gain_attend, shift_attend, gain_hidden, shift_hidden], axis=1)
    vectors = jnp.pad(vectors, ((0, 0), (0, 59)))

    def for_member(which):
        piece = lax.dynamic_index_in_dim(columns, which, 0, keepdims=False)
        return jnp.concatenate([piece, vectors], axis=1)

    def ordered(which, low_piece, high_piece):
        return jnp.where(
            which,
            jnp.concatenate([high_piece, low_piece]),
            jnp.concatenate([low_piece, high_piece]),
        )

    def is_upper(bit):
        return ((row >> bit) & 1) == 1

    def flipped(mask):
        return lambda d, z: (d ^ mask, z)

    bits = dp.bit_length() - 1
    own = for_member(member)[None]
    gathered = ordered(is_upper(0), own, send(for_member(member ^ 2), other_core)[None])
    bit = 1
    while bit < bits:
        near = ordered(is_upper(bit), gathered, send(gathered, flipped(1 << bit)))
        if bit + 1 < bits:
            far = ordered(
                is_upper(bit),
                send(gathered, flipped(2 << bit)),
                send(gathered, flipped(3 << bit)),
            )
            near = ordered(is_upper(bit + 1), near, far)
        gathered = near
        bit += 2
    first, gathered = together(first, gathered)
    wt = gathered.reshape(model, 3 * width + 64).T
    late = send(first, lambda d, z: None if at_home(d, z) else (d, z ^ 1))
    first_other = send(first, other_core)

    pack = jnp.concatenate(
        [hidden_down]
        + [hidden_up[:, k * model : (k + 1) * model] for k in range(groups)]
        + [attend_out]
    )
    height = pack.shape[0]
    weights = lax.all_gather(pack, "dp", axis=0, tiled=False)
    split = dp if (model // dp) % 96 == 0 else 1
    if split == 1:
        tall = hidden_down.shape[0]
        down = weights[:, :tall].reshape(1, dp * tall, model)
        others = weights[:, tall:].reshape(dp, groups + 1, share, model).transpose(1, 0, 2, 3)
        weights = jnp.concatenate([down, others.reshape(1, -1, model)], axis=1)

    stay_flag = stays.astype(jnp.int32)
    early = jnp.where(stays, member, member ^ 2)
    info = jnp.stack([stay_flag, member, core]).astype(jnp.int32)
    info_early = jnp.stack([stay_flag, early, early ^ 1, early ^ 2]).astype(jnp.int32)
    info_late = jnp.stack([stay_flag, early ^ 3]).astype(jnp.int32)
    carried = project(
        info_early, [mine, mine_other, first, first_other, first_other, first], wt, None
    )
    late, packed, grad_mine = together(late, carried[0], cotangent[0])
    late_other = send(late, other_core)
    packed, normed = project(info_late, [late_other, late], wt, [packed, carried[1]])
    grad_moved = send(grad_mine, swap)

    *outs, logsum = attend_forward(info, packed)
    mine, first, logsum = together(mine, first, logsum)
    routes = [None, next_chip, other_core, lambda d, z: (d ^ 1, z ^ 1)]
    merged = [outs[0]] + [send(outs[j], routes[j]) for j in (1, 3, 2)]
    merged = [merged[0], merged[1], merged[3], merged[2]]

    tokens = jnp.where(stays, mine, first)
    cot = jnp.where(stays, grad_mine, grad_moved)
    layer_out, resid_grad, a0, a1, a2, a3, stats, down_own, down_other, grads = hidden_layer(
        info, tokens, cot, merged, wt, weights, groups
    )
    r1 = send(a1, routes[1])
    r3 = send(a3, routes[3])
    r2 = send(a2, routes[2])
    if split == 1:
        grads = grads[0].reshape(groups + 1, dp, share, model).transpose(1, 0, 2, 3)
        grads = grads.reshape(dp, (groups + 1) * share, model)
        down_pieces = [
            lax.psum_scatter(
                down_own.reshape(dp, -1, model), "dp", scatter_dimension=0, tiled=True
            )[0]
        ]
    else:
        down_got = send(down_other, other_core)
        chip = row >> 1

        def down_piece(j):
            mine_at = [
                lax.dynamic_index_in_dim(v, chip ^ j, 0, keepdims=False).astype(F32)
                for v in (down_own, down_got)
            ]
            return (mine_at[0] + mine_at[1]).astype(BF)

        down_pieces = [down_piece(0)]
        down_pieces += [send(down_piece(j), flipped(j << 1)) for j in range(1, dp // 2)]
    reduced = lax.psum_scatter(grads, "dp", scatter_dimension=0, tiled=True)[0]

    layer_out, r3 = together(layer_out, r3)
    layer_moved = send(layer_out, swap)
    def to_owner(value, owner):
        return send(value, lambda d, z: None if (d & 1) == owner else (d ^ 1, z))

    def to_chip(value, owner):
        return send(value, lambda d, z: (d, z ^ 1) if (d & 1) == owner else None)

    def home_from(owner):
        return lambda d, z: None if at_home(d, z) or (d & 1) != owner else (d ^ 1, z ^ 2)

    all_grads = [a0, r1, r2, r3]
    near, far, stacked, *state = attend_backward(info, packed, outs, all_grads, logsum, wt)
    near, far, layer_moved, *down_pieces = together(near, far, layer_moved, *down_pieces)
    down_sum = sum([p.astype(F32) for p in down_pieces[1:]], down_pieces[0].astype(F32))
    down_sum = down_sum.astype(BF)
    far_other, near_other = to_owner(far, 1), to_owner(near, 1)
    partial = (far.astype(F32) + far_other.astype(F32)).astype(BF)
    partial, stacked = together(partial, stacked)
    far_chip = to_chip(partial, 1)
    dw = project_grad(stacked, normed, 1)
    state[0], dw, reduced = together(state[0], dw, reduced)
    reduced = jnp.concatenate([down_sum, reduced])
    scattered = lax.psum_scatter(reduced, "seq", scatter_dimension=0, tiled=True)
    near_b, far_b, stacked = attend_backward(
        info, packed, outs, all_grads, logsum, wt, state
    )
    far_chip, far_b, near_b = together(far_chip, far_b, near_b)
    far_b_other, near_b_other = to_owner(far_b, 0), to_owner(near_b, 0)
    far_b_other, scattered = together(far_b_other, scattered)
    partial = (far_b.astype(F32) + far_b_other.astype(F32)).astype(BF)
    partial, stacked, far_chip = together(partial, stacked, far_chip)
    far_b_chip = to_chip(partial, 0)
    input_grad, low_a, stats = final_norm(
        1, info, tokens, [near, near_other, far_chip], resid_grad, wt, stats
    )
    dw = project_grad(stacked, normed, 0, dw)
    far_b_chip, scattered, low_a, dw = together(far_b_chip, scattered, low_a, dw)
    moved_a = send(low_a, home_from(1))
    total = lax.all_gather(scattered, "seq", axis=0, tiled=True)
    input_grad, low_b, stats = final_norm(
        0, info, tokens, [near_b, near_b_other, far_b_chip], resid_grad, wt, stats, input_grad
    )
    moved_b = send(low_b, home_from(0))

    small = jnp.pad(stats.T, ((0, 0), (0, 56))).astype(BF)
    current = jnp.concatenate([dw, small], axis=1).reshape(dp, share, 3 * width + 64)
    top = bits - 1
    while top > 0:
        width_bits = 2 if top > 1 else 1
        quarter = current.shape[0] >> width_bits
        low_bit = top - width_bits + 1
        mine_at = (row >> low_bit) & ((1 << width_bits) - 1)

        def piece(j):
            return lax.dynamic_slice_in_dim(current, (mine_at ^ j) * quarter, quarter, 0)

        pieces = [piece(0)]
        pieces += [send(piece(j), flipped(j << low_bit)) for j in range(1, 1 << width_bits)]
        moved_a, *pieces = together(moved_a, *pieces)
        summed = sum([p.astype(F32) for p in pieces[1:]], pieces[0].astype(F32))
        current = summed.astype(BF)
        top -= width_bits
    got = send(current, lambda d, z: (d, z ^ 2))
    got, moved_b, total = together(got, moved_b, total)
    input_moved = jnp.where(core == 0, moved_a, moved_b)
    current = (current.astype(F32) + got.astype(F32)).astype(BF)
    upper = core == 1
    give = jnp.where(upper, current[0], current[1])
    keep = jnp.where(upper, current[1], current[0])
    got = send(give, other_core)
    pair = jnp.where(upper, jnp.stack([got, keep]), jnp.stack([keep, got]))
    far = send(pair, next_chip)
    odd = (line & 1) == 1
    quad = [
        jnp.where(odd, far[0], pair[0]),
        jnp.where(odd, pair[0], far[0]),
        jnp.where(odd, far[1], pair[1]),
        jnp.where(odd, pair[1], far[1]),
    ]
    proj_grad = jnp.concatenate(
        [q[:, p * width : (p + 1) * width] for p in range(3) for q in quad], axis=1
    ).astype(F32)
    small = sum([q[:, 3 * width :].astype(F32) for q in quad[1:]], quad[0][:, 3 * width :].astype(F32))
    small = small.T
    total = total.astype(F32)

    tall = hidden_down.shape[0]
    down_grad = total[:tall]
    up_grad = jnp.concatenate(
        [total[tall + k * share : tall + (k + 1) * share] for k in range(groups)], axis=1
    )
    out_grad = total[tall + groups * share :]
    return (
        jnp.where(stays, layer_out, layer_moved)[None],
        jnp.where(stays, input_grad, input_moved.astype(F32))[None],
        small[4],
        small[2],
        small[3],
        proj_grad,
        out_grad,
        small[0],
        small[1],
        up_grad,
        down_grad,
    )


def solution(mesh):
    vector, matrix, tokens = P("dp"), P("dp", None), P("dp", "seq", None)
    return jax.shard_map(
        functools.partial(on_device, mesh.shape["dp"]),
        mesh=mesh,
        in_specs=(
            tokens,
            vector,
            vector,
            vector,
            matrix,
            matrix,
            vector,
            vector,
            matrix,
            matrix,
            tokens,
        ),
        out_specs=(
            tokens,
            tokens,
            vector,
            vector,
            vector,
            matrix,
            matrix,
            vector,
            vector,
            matrix,
            matrix,
        ),
        check_vma=False,
    )
```

```python
import functools

import jax
import jax.numpy as jnp
from jax import lax
from jax.experimental import pallas as pl
from jax.experimental.pallas import tpu as pltpu
from jax.sharding import PartitionSpec as P

HD = 64
EPSILON = 1e-05
MASKED = -1e30
F32 = jnp.float32
BF = jnp.bfloat16
MEMBERS = 4
VMEM_LIMIT = 60 << 20
GELU_A = 0.7978845608028654
GELU_B = 0.044715


def contract(left, right, left_dim, right_dim):
    return lax.dot_general(
        left, right, (((left_dim,), (right_dim,)), ((), ())), preferred_element_type=F32
    )


def normalize(hidden):
    center = hidden - jnp.mean(hidden, axis=-1, keepdims=True)
    spread = jnp.mean(center * center, axis=-1, keepdims=True)
    inverse = lax.rsqrt(spread + EPSILON)
    return center * inverse, inverse


def norm_backward(grad, gain, unit, inverse):
    scaled = grad * gain
    return inverse * (
        scaled
        - jnp.mean(scaled, axis=-1, keepdims=True)
        - unit * jnp.mean(scaled * unit, axis=-1, keepdims=True)
    )


def in_hbm(*values):
    return [pltpu.with_memory_space_constraint(v, pltpu.HBM) for v in values]


def params(*semantics, limit=VMEM_LIMIT):
    return pltpu.CompilerParams(dimension_semantics=semantics, vmem_limit_bytes=limit)


def whole(shape):
    zeros = (0,) * len(shape)
    return pl.BlockSpec(shape, lambda *_: zeros, pipeline_mode=pl.Buffered(1))


def project_body(count, info, *refs):
    sources, wt = refs[: 2 * count], refs[2 * count]
    packed, normed = refs[-2:]
    slot = pl.program_id(0)
    stay = info[0] > 0
    cols = wt.shape[0] - 64
    vec = wt[cols : cols + 8, :].astype(F32)
    for which in range(count):
        for wanted in (True, False):
            source = sources[2 * which + (0 if wanted else 1)]

            @pl.when(jnp.logical_and(slot == which, stay == wanted))
            def _(source=source):
                unit, _ = normalize(source[...].astype(F32) + vec[0:1])
                normed[...] = (unit * vec[1:2] + vec[2:3]).astype(BF)

    packed[...] = contract(wt[:cols, :], normed[...], 1, 1).astype(BF)


def project(info, sources, wt, carried, rows=384):
    chunk, width = sources[0].shape
    count = len(sources) // 2
    cols = wt.shape[0] - 64
    length = MEMBERS * chunk
    per = chunk // rows

    def src(which, wanted):
        def index(s, b, info):
            block = jnp.where(s == which, b, (per - 1) * (s > which))
            return (jnp.where(info[0] == wanted, block, 0), 0)

        return pl.BlockSpec((rows, width), index)

    def place(s, b, info):
        return info[1 + s] * per + b

    in_specs = [src(w, f) for w in range(count) for f in (1, 0)] + [whole(wt.shape)]
    aliases = {}
    args = [info, *in_hbm(*sources), wt]
    if carried is not None:
        in_specs += [pl.BlockSpec(memory_space=pl.ANY)] * 2
        aliases = {2 * count + 2: 0, 2 * count + 3: 1}
        args += list(carried)
    return pl.pallas_call(
        functools.partial(project_body, count),
        grid_spec=pltpu.PrefetchScalarGridSpec(
            num_scalar_prefetch=1,
            grid=(count, per),
            in_specs=in_specs,
            out_specs=[
                pl.BlockSpec((cols, rows), lambda s, b, info: (0, place(s, b, info))),
                pl.BlockSpec((rows, width), lambda s, b, info: (place(s, b, info), 0)),
            ],
        ),
        out_shape=[
            jax.ShapeDtypeStruct((cols, length), BF),
            jax.ShapeDtypeStruct((length, width), BF),
        ],
        input_output_aliases=aliases,
        compiler_params=params("arbitrary", "arbitrary"),
        cost_estimate=pl.CostEstimate(
            flops=2 * count * chunk * width * cols,
            transcendentals=count * chunk,
            bytes_accessed=6 * count * chunk * width,
        ),
        name="norm_project",
    )(*args)


def diagonal(size):
    key = lax.broadcasted_iota(jnp.int32, (size, size), 0)
    query = lax.broadcasted_iota(jnp.int32, (size, size), 1)
    return key <= query


def forward_body(heads, info, packed, out0, out1, out2, out3, logsum, keys):
    step = pl.program_id(0)
    width = heads * HD
    size = out0.shape[1]
    scale = BF(HD**-0.5)

    @pl.when(step == 0)
    def _():
        for h in range(heads):
            keys[h] = packed[width + h * HD : width + (h + 1) * HD, :].T

    first = pl.multiple_of(step * size, size)
    queries = [packed[h * HD : (h + 1) * HD, pl.ds(first, size)] * scale for h in range(heads)]

    def block(span, carry, allowed, part):
        all_scores = [
            contract(keys[h, span, :], queries[h][:, part], 1, 0) for h in range(heads)
        ]
        result = []
        for h in range(heads):
            top, total, summed = carry[h]
            scores = all_scores[h]
            if allowed is not None:
                scores = jnp.where(allowed, scores, MASKED)
            new_top = jnp.maximum(top, jnp.max(scores, axis=0, keepdims=True))
            weights = jnp.exp(scores - new_top)
            shrink = jnp.exp(top - new_top)
            total = total * shrink + jnp.sum(weights, axis=0, keepdims=True)
            values = packed[2 * width + h * HD : 2 * width + (h + 1) * HD, span]
            summed = summed * shrink + contract(values, weights.astype(BF), 1, 0)
            result.append((new_top, total, summed))
        return tuple(result)

    begin = tuple(
        (
            jnp.full((1, size), MASKED, F32),
            jnp.zeros((1, size), F32),
            jnp.zeros((HD, size), F32),
        )
        for _ in range(heads)
    )
    carry = lax.fori_loop(
        0,
        step,
        lambda j, c: block(pl.ds(pl.multiple_of(j * size, size), size), c, None, slice(0, size)),
        begin,
    )
    half = size // 2
    lower, upper = pl.ds(first, half), pl.ds(pl.multiple_of(first + half, half), half)
    allowed = diagonal(half)
    left = [tuple(v[:, :half] for v in c) for c in carry]
    right = [tuple(v[:, half:] for v in c) for c in carry]
    left = block(lower, left, allowed, slice(0, half))
    right = block(lower, right, None, slice(half, size))
    right = block(upper, right, allowed, slice(half, size))
    carry = [
        tuple(jnp.concatenate([a, b], axis=1) for a, b in zip(l, r)) for l, r in zip(left, right)
    ]
    place = step ^ info[1]
    for h in range(heads):
        top, total, summed = carry[h]
        logsum[h : h + 1, :] = top + jnp.log(total)
        low = (summed / total).astype(BF)
        for j, out in enumerate((out0, out1, out2, out3)):

            @pl.when(place == j)
            def _(out=out, low=low, h=h):
                out[h * HD : (h + 1) * HD, :] = low


def attend_forward(info, packed):
    cols, length = packed.shape
    heads = cols // (3 * HD)
    width = heads * HD
    size = length // MEMBERS
    part = jax.ShapeDtypeStruct((width, size), BF)
    return pl.pallas_call(
        functools.partial(forward_body, heads),
        grid_spec=pltpu.PrefetchScalarGridSpec(
            num_scalar_prefetch=1,
            grid=(MEMBERS,),
            in_specs=[whole(packed.shape)],
            out_specs=[pl.BlockSpec((width, size), lambda s, info: (0, 0))] * MEMBERS
            + [pl.BlockSpec((8, size), lambda s, info: (0, s))],
            scratch_shapes=[pltpu.VMEM((heads, length, HD), BF)],
        ),
        out_shape=[part] * MEMBERS + [jax.ShapeDtypeStruct((8, length), F32)],
        compiler_params=params("arbitrary"),
        cost_estimate=pl.CostEstimate(
            flops=heads * length * HD, transcendentals=length, bytes_accessed=width * length
        ),
        name="attention_forward",
    )(info, packed)


def backward_body(heads, top, info, packed, o0, o1, o2, o3, g0, g1, g2, g3, logsum, wt, *rest):
    last_stage = top == 1
    keys, values, grad_keys, grad_values, out_all, grad_all = rest[-6:]
    if last_stage:
        keys_in, values_in, near, far, stacked_out = rest[:-6]
    else:
        near, far, stacked_out, keys_out, values_out = rest[:-6]
    step = pl.program_id(0)
    chunk_id = top - step
    width = heads * HD
    size = near.shape[0]
    scale = BF(HD**-0.5)

    @pl.when(step == 0)
    def _():
        for h in range(heads):
            keys[h] = packed[width + h * HD : width + (h + 1) * HD, :].T
            values[h] = packed[2 * width + h * HD : 2 * width + (h + 1) * HD, :].T
        if last_stage:
            grad_keys[...] = keys_in[...]
            grad_values[...] = values_in[...]
        else:
            grad_keys[...] = jnp.zeros_like(grad_keys)
            grad_values[...] = jnp.zeros_like(grad_values)
        for j, (o, g) in enumerate(((o0, g0), (o1, g1), (o2, g2), (o3, g3))):
            out_all[info[1] ^ j] = o[...]
            grad_all[info[1] ^ j] = g[...]

    first = pl.multiple_of(chunk_id * size, size)
    rows = [slice(h * HD, (h + 1) * HD) for h in range(heads)]
    query_t = [packed[r, pl.ds(first, size)] * scale for r in rows]
    query = [q.T for q in query_t]
    grad_t = [grad_all[chunk_id, r, :] for r in rows]
    grad = [g.T for g in grad_t]
    delta = [
        jnp.sum(g.astype(F32) * out_all[chunk_id, r, :].astype(F32), axis=0, keepdims=True)
        for g, r in zip(grad_t, rows)
    ]
    lse = [logsum[h : h + 1, :] for h in range(heads)]

    def block(span, carry, allowed, part):
        result = []
        for h in range(heads):
            scores = contract(keys[h, span, :], query_t[h][:, part], 1, 0)
            grad_probs = contract(values[h, span, :], grad_t[h][:, part], 1, 0)
            probs = jnp.exp(scores - lse[h][:, part])
            if allowed is not None:
                probs = jnp.where(allowed, probs, 0.0)
            grad_scores = (probs * (grad_probs - delta[h][:, part])).astype(BF)
            grad_values[h, span, :] += contract(probs.astype(BF), grad[h][part], 1, 0)
            grad_keys[h, span, :] += contract(grad_scores, query[h][part], 1, 0)
            keys_t = packed[width + h * HD : width + (h + 1) * HD, span]
            result.append(carry[h] + contract(keys_t, grad_scores, 1, 0))
        return tuple(result)

    grad_query = tuple(jnp.zeros((HD, size), F32) for _ in range(heads))
    grad_query = lax.fori_loop(
        0,
        chunk_id,
        lambda j, c: block(pl.ds(pl.multiple_of(j * size, size), size), c, None, slice(0, size)),
        grad_query,
    )
    half = size // 2
    lower, upper = pl.ds(first, half), pl.ds(pl.multiple_of(first + half, half), half)
    allowed = diagonal(half)
    left = block(lower, [g[:, :half] for g in grad_query], allowed, slice(0, half))
    right = block(lower, [g[:, half:] for g in grad_query], None, slice(half, size))
    right = block(upper, right, allowed, slice(half, size))
    grad_query = [jnp.concatenate([a, b], axis=1) for a, b in zip(left, right)]
    pieces = [(g * HD**-0.5).astype(BF) for g in grad_query]
    pieces += [grad_keys[h, pl.ds(first, size), :].astype(BF).T for h in range(heads)]
    pieces += [grad_values[h, pl.ds(first, size), :].astype(BF).T for h in range(heads)]
    stacked = jnp.concatenate(pieces, axis=0)
    partial = contract(stacked, wt[: 3 * width, :], 0, 0).astype(BF)
    is_near = ((chunk_id ^ info[1]) & 1) == 0

    @pl.when(is_near)
    def _():
        near[...] = partial

    @pl.when(jnp.logical_not(is_near))
    def _():
        far[...] = partial

    stacked_out[...] = stacked
    if not last_stage:

        @pl.when(step == 1)
        def _():
            left = keys_out.shape[1]
            keys_out[...] = grad_keys[:, :left, :]
            values_out[...] = grad_values[:, :left, :]


def attend_backward(info, packed, outs, grads, logsum, wt, carried=None):
    cols, length = packed.shape
    heads = cols // (3 * HD)
    width = heads * HD
    size = length // MEMBERS
    model = wt.shape[1]
    top = MEMBERS - 1 if carried is None else 1
    span = (top + 1) * size
    left = length // 2

    def fixed(shape):
        zeros = (0,) * len(shape)
        return pl.BlockSpec(shape, lambda s, info: zeros)

    partial = jax.ShapeDtypeStruct((size, model), BF)
    state = jax.ShapeDtypeStruct((heads, left, HD), F32)
    in_specs = (
        [whole((cols, span))]
        + [whole((width, size))] * (2 * MEMBERS)
        + [
            pl.BlockSpec((8, size), lambda s, info: (0, top - s)),
            whole(wt.shape),
        ]
    )
    out_shape = [partial, partial, jax.ShapeDtypeStruct((cols, 2 * size), BF)]
    out_specs = [fixed((size, model))] * 2
    out_specs += [pl.BlockSpec((cols, size), lambda s, info: (0, 1 - s))]
    if carried is None:
        more = ()
        out_shape += [state, state]
        out_specs += [fixed(state.shape)] * 2
    else:
        more = tuple(carried)
        in_specs += [whole(state.shape)] * 2
    blocks = 7 if carried is None else 3
    return pl.pallas_call(
        functools.partial(backward_body, heads, top),
        grid_spec=pltpu.PrefetchScalarGridSpec(
            num_scalar_prefetch=1,
            grid=(2,),
            in_specs=in_specs,
            out_specs=out_specs,
            scratch_shapes=[
                pltpu.VMEM((heads, span, HD), BF),
                pltpu.VMEM((heads, span, HD), BF),
                pltpu.VMEM((heads, span, HD), F32),
                pltpu.VMEM((heads, span, HD), F32),
                pltpu.VMEM((MEMBERS, width, size), BF),
                pltpu.VMEM((MEMBERS, width, size), BF),
            ],
        ),
        out_shape=out_shape,
        compiler_params=params("arbitrary"),
        cost_estimate=pl.CostEstimate(
            flops=200 * heads * blocks * size * size * HD,
            transcendentals=heads * blocks * size * size,
            bytes_accessed=20 * width * length,
        ),
        name="attention_backward",
    )(info, packed, *in_hbm(*outs, *grads), logsum, wt, *more)


def project_grad_body(*refs):
    stacked, normed = refs[:2]
    out, total = refs[-2:]
    step = pl.program_id(0)
    part = contract(stacked[...], normed[...], 1, 0)

    @pl.when(step == 0)
    def _():
        total[...] = part if len(refs) == 4 else refs[2][...] + part

    @pl.when(step == 1)
    def _():
        if len(refs) == 4:
            out[...] = total[...] + part
        else:
            out[...] = (total[...] + part).astype(BF).T


def project_grad(stacked, normed, half, before=None):
    cols, span = stacked.shape
    size = span // 2
    model = normed.shape[1]
    more = () if before is None else (before,)
    if before is None:
        out = jax.ShapeDtypeStruct((cols, model), F32)
    else:
        out = jax.ShapeDtypeStruct((model, cols), BF)
    return pl.pallas_call(
        project_grad_body,
        grid=(2,),
        in_specs=[
            pl.BlockSpec((cols, size), lambda s: (0, s)),
            pl.BlockSpec((size, model), lambda s: (2 * half + s, 0)),
        ]
        + [whole((cols, model))] * len(more),
        out_specs=pl.BlockSpec(out.shape, lambda s: (0, 0)),
        out_shape=out,
        scratch_shapes=[pltpu.VMEM((cols, model), F32)],
        compiler_params=params("arbitrary", limit=24 << 20),
        cost_estimate=pl.CostEstimate(
            flops=2 * cols * span * model, transcendentals=0, bytes_accessed=2 * span * (cols + model)
        ),
        name="project_grad",
    )(stacked, normed, *more)


def hidden_body(groups, rows, info, tok, cot, m0, m1, m2, m3, vec_ref, down_ref, up_ref, out_w, *rest):
    (
        layer_out, resid_grad, a0, a1, a2, a3, stats, down_own, down_other, grads,
        low, unit, inverse, result, grad_n, act, grad_pre, stage, sems,
    ) = rest
    step = pl.program_id(0)
    member = info[1]
    vec = vec_ref[0:8, :].astype(F32)
    size, model = tok.shape
    width = model // MEMBERS
    units, piece = stage.shape[1], stage.shape[2]
    split = grads.shape[0]
    share = units // MEMBERS

    def out_rows(j):
        if split == 1:
            return out_w[0, pl.ds(pl.multiple_of((member ^ j) * width, width), width), :]
        unit_rows = out_w.shape[1]
        count = width // unit_rows
        return out_w[pl.ds((member ^ j) * count, count)].reshape(width, model)

    def drain(slot):
        pltpu.make_async_copy(stage.at[slot], stage.at[slot], sems.at[slot]).wait()

    def put_down(slot, block):
        for b in range(units):
            source = stage.at[slot, b]
            if split == 1:
                start = pl.multiple_of(block * model + b * piece, 16)
                target = down_own.at[0, pl.ds(start, piece), :]
                pltpu.make_async_copy(source, target, sems.at[slot]).start()
                continue
            per = units // 2
            rows_at = slice((b % per) * piece, (b % per + 1) * piece)
            for wanted, array in ((True, down_own), (False, down_other)):

                @pl.when((info[2] == b // per) == wanted)
                def _(array=array, source=source, rows_at=rows_at):
                    target = array.at[block, rows_at, :]
                    pltpu.make_async_copy(source, target, sems.at[slot]).start()

    def put(slot, block):
        for b in range(units):
            if split == 1:
                row, start = 0, block * model + b * piece
            else:
                row, start = b, block * piece
            if not isinstance(start, int):
                start = pl.multiple_of(start, 16)
            pltpu.make_async_copy(
                stage.at[slot, b], grads.at[row, pl.ds(start, piece), :], sems.at[slot]
            ).start()

    @pl.when(step == 0)
    def _():
        branch = None
        for j, merged in enumerate((m0, m1, m2, m3)):
            part = contract(merged[...], out_rows(j), 0, 0)
            branch = part if branch is None else branch + part
        resid = tok[...].astype(F32) + vec[0:1] + branch
        normal, spread = normalize(resid)
        low[...] = (normal * vec[3:4] + vec[4:5]).astype(BF)
        unit[...] = normal
        inverse[...] = spread
        result[...] = resid
        grad_n[...] = jnp.zeros_like(grad_n)

    up = up_ref[...].reshape(model, model)
    down = down_ref[...].reshape(model, model)

    def tile(i, _):
        span = pl.ds(pl.multiple_of(i * rows, rows), rows)
        pre = contract(low[span, :], up, 1, 0)
        grad_act = contract(cot[span, :], down, 1, 1)
        square = pre * pre
        half = 0.5 + 0.5 * jnp.tanh(pre * (GELU_A + GELU_A * GELU_B * square))
        gelu = pre * half
        act_low = gelu.astype(BF)
        act[span, :] = act_low
        slope = half + gelu * (1.0 - half) * (2.0 * GELU_A + 6.0 * GELU_A * GELU_B * square)
        grad_low = (grad_act * slope).astype(BF)
        grad_pre[span, :] = grad_low
        result[span, :] += contract(act_low, down, 1, 0)
        grad_n[span, :] += contract(grad_low, up, 1, 1)
        return 0

    if rows == size:
        tile(0, 0)
    else:
        lax.fori_loop(0, size // rows, tile, 0)

    slot = 2 * (step % 2)

    @pl.when(step >= 2)
    def _():
        drain(slot)
        drain(slot + 1)

    stage[slot] = contract(act[...], cot[...], 0, 0).astype(BF).reshape(units, piece, model)
    put_down(slot, step)
    stage[slot + 1] = contract(low[...], grad_pre[...], 0, 0).astype(BF).reshape(units, piece, model)
    put(slot + 1, step)

    @pl.when(step == groups - 1)
    def _():
        layer_out[...] = result[...].astype(BF)
        grad = grad_n[...]
        total = cot[...].astype(F32) + norm_backward(grad, vec[3:4], unit[...], inverse[...])
        resid_grad[...] = total
        branch = total.astype(BF)
        for j, out in enumerate((a0, a1, a2, a3)):
            out[...] = contract(out_rows(j), branch, 1, 1).astype(BF)
        stats[...] = jnp.zeros_like(stats)
        stats[0:1, :] = jnp.sum(grad * unit[...], axis=0, keepdims=True)
        stats[1:2, :] = jnp.sum(grad, axis=0, keepdims=True)
        other = 2 * (groups % 2)
        drain(other)
        for j, merged in enumerate((m0, m1, m2, m3)):
            block = contract(merged[...], branch, 1, 0).astype(BF)
            stage[other, pl.ds((member ^ j) * share, share)] = block.reshape(share, piece, model)
        put(other, groups)
        for which in range(4):
            drain(which)


def hidden_layer(info, tok, cot, merged, wt, weights, groups, rows=768):
    size, model = tok.shape
    width = model // MEMBERS
    split, height, _ = weights.shape
    unit = model // split
    tall = height - (groups + 1) * unit
    units = 8
    vec_block = wt.shape[0] // 64 - 1
    down_shape = (1, tall, model) if split == 1 else (split // 2, tall, model)
    if split == 1:
        down_spec = pl.BlockSpec((1, model, model), lambda k, info: (0, k, 0))
        up_spec = pl.BlockSpec((1, model, model), lambda k, info: (0, groups + k, 0))
        out_spec = pl.BlockSpec(
            (1, model, model), lambda k, info: (0, 2 * groups, 0), pipeline_mode=pl.Buffered(1)
        )
    else:
        base = tall // unit
        down_spec = pl.BlockSpec((model // tall, tall, model), lambda k, info: (k, 0, 0))
        up_spec = pl.BlockSpec((split, unit, model), lambda k, info: (0, base + k, 0))
        out_spec = pl.BlockSpec(
            (split, unit, model),
            lambda k, info: (0, base + groups, 0),
            pipeline_mode=pl.Buffered(1),
        )

    def fixed(shape):
        zeros = (0,) * len(shape)
        return pl.BlockSpec(shape, lambda k, info: zeros)

    def shaped(shape, dtype):
        return jax.ShapeDtypeStruct(shape, dtype)

    return pl.pallas_call(
        functools.partial(hidden_body, groups, rows),
        grid_spec=pltpu.PrefetchScalarGridSpec(
            num_scalar_prefetch=1,
            grid=(groups,),
            in_specs=[whole((size, model))] * 2
            + [whole((width, size))] * MEMBERS
            + [
                pl.BlockSpec((64, model), lambda k, info: (vec_block, 0)),
                down_spec,
                up_spec,
                out_spec,
            ],
            out_specs=[fixed((size, model))] * 2
            + [fixed((width, size))] * MEMBERS
            + [fixed((8, model))]
            + [pl.BlockSpec(memory_space=pl.ANY)] * 3,
            scratch_shapes=[
                pltpu.VMEM((size, model), BF),
                pltpu.VMEM((size, model), F32),
                pltpu.VMEM((size, 1), F32),
                pltpu.VMEM((size, model), F32),
                pltpu.VMEM((size, model), F32),
                pltpu.VMEM((size, model), BF),
                pltpu.VMEM((size, model), BF),
                pltpu.VMEM((4, units, model // units, model), BF),
                pltpu.SemaphoreType.DMA((4,)),
            ],
        ),
        out_shape=[shaped((size, model), BF), shaped((size, model), F32)]
        + [shaped((width, size), BF)] * MEMBERS
        + [
            shaped((8, model), F32),
            shaped(down_shape, BF),
            shaped(down_shape if split > 1 else (1, 16, model), BF),
            shaped((split, (groups + 1) * unit, model), BF),
        ],
        compiler_params=params("arbitrary"),
        cost_estimate=pl.CostEstimate(
            flops=6 * size * model * (2 * groups + 1) * model,
            transcendentals=size * groups * model,
            bytes_accessed=4 * weights.size + 12 * size * model,
        ),
        name="hidden_layer",
    )(info, *in_hbm(tok, cot, *merged), wt, weights, weights, weights)


def final_body(owner, info, tok, p0, p1, p2, resid_grad, vec_ref, before, *rest):
    out, low, stats = rest[-3:]
    step = pl.program_id(0)
    mine = info[2] == owner
    vec = vec_ref[0:8, :].astype(F32)

    @pl.when(step == 0)
    def _():
        stats[...] = before[...]

    @pl.when(mine)
    def _():
        unit, inverse = normalize(tok[...].astype(F32) + vec[0:1])
        grad = p0[...].astype(F32) + p1[...].astype(F32) + p2[...].astype(F32)
        result = resid_grad[...] + norm_backward(grad, vec[1:2], unit, inverse)
        out[...] = result
        low[...] = result.astype(BF)
        stats[2:3, :] += jnp.sum(grad * unit, axis=0, keepdims=True)
        stats[3:4, :] += jnp.sum(grad, axis=0, keepdims=True)
        stats[4:5, :] += jnp.sum(result, axis=0, keepdims=True)

    if len(rest) == 4:

        @pl.when(jnp.logical_not(mine))
        def _():
            out[...] = rest[0][...]


def final_norm(owner, info, tokens, parts, resid_grad, wt, before, earlier=None, rows=384):
    size, model = tokens.shape
    tok = pl.BlockSpec((rows, model), lambda s, info: (s, 0))
    one = pl.BlockSpec((8, model), lambda s, info: (0, 0))
    vec_block = wt.shape[0] // 64 - 1
    more = () if earlier is None else (earlier,)
    return pl.pallas_call(
        functools.partial(final_body, owner),
        grid_spec=pltpu.PrefetchScalarGridSpec(
            num_scalar_prefetch=1,
            grid=(size // rows,),
            in_specs=[tok] * 5
            + [pl.BlockSpec((64, model), lambda s, info: (vec_block, 0)), one]
            + [tok] * len(more),
            out_specs=[tok, tok, one],
        ),
        out_shape=[
            jax.ShapeDtypeStruct((size, model), F32),
            jax.ShapeDtypeStruct((size, model), BF),
            jax.ShapeDtypeStruct((8, model), F32),
        ],
        compiler_params=params("arbitrary"),
        cost_estimate=pl.CostEstimate(
            flops=size * model, transcendentals=size, bytes_accessed=size * model
        ),
        name="final_norm",
    )(info, *in_hbm(tokens, *parts, resid_grad), wt, before, *more)


def together(*values):
    return lax.optimization_barrier(values)


def on_device(
    groups_dp,
    inputs,
    pass_embed,
    gain_attend,
    shift_attend,
    attend_in,
    attend_out,
    gain_hidden,
    shift_hidden,
    hidden_up,
    hidden_down,
    cotangent,
):
    axes = ("dp", "seq")
    dp = groups_dp
    row = lax.axis_index("dp")
    line = lax.axis_index("seq")
    core = row & 1
    stays = core == (line >> 1)
    member = core * 2 + (line & 1)
    model = inputs.shape[2]
    width = model // MEMBERS
    share = attend_in.shape[0]
    groups = hidden_up.shape[1] // model

    def send(value, target):
        pairs = []
        for d in range(dp):
            for z in range(MEMBERS):
                goal = target(d, z)
                if goal is not None:
                    pairs.append((d * MEMBERS + z, goal[0] * MEMBERS + goal[1]))
        return lax.ppermute(value, axes, pairs)

    def at_home(d, z):
        return (d & 1) == (z >> 1)

    def swap(d, z):
        return None if at_home(d, z) else (d ^ 1, z ^ 2)

    def other_core(d, z):
        return (d ^ 1, z)

    def next_chip(d, z):
        return (d, z ^ 1)

    mine = inputs[0]
    first = send(mine, lambda d, z: (d, z ^ 1) if at_home(d, z) else (d ^ 1, z ^ 2))
    mine_other = send(mine, other_core)

    columns = attend_in.reshape(share, 3, MEMBERS, width).transpose(2, 0, 1, 3)
    columns = columns.reshape(MEMBERS, share, 3 * width)
    vectors = jnp.stack([pass_embed, gain_attend, shift_attend, gain_hidden, shift_hidden], axis=1)
    vectors = jnp.pad(vectors, ((0, 0), (0, 59)))

    def for_member(which):
        piece = lax.dynamic_index_in_dim(columns, which, 0, keepdims=False)
        return jnp.concatenate([piece, vectors], axis=1)

    def ordered(which, low_piece, high_piece):
        return jnp.where(
            which,
            jnp.concatenate([high_piece, low_piece]),
            jnp.concatenate([low_piece, high_piece]),
        )

    def is_upper(bit):
        return ((row >> bit) & 1) == 1

    def flipped(mask):
        return lambda d, z: (d ^ mask, z)

    bits = dp.bit_length() - 1
    own = for_member(member)[None]
    gathered = ordered(is_upper(0), own, send(for_member(member ^ 2), other_core)[None])
    bit = 1
    while bit < bits:
        near = ordered(is_upper(bit), gathered, send(gathered, flipped(1 << bit)))
        if bit + 1 < bits:
            far = ordered(
                is_upper(bit),
                send(gathered, flipped(2 << bit)),
                send(gathered, flipped(3 << bit)),
            )
            near = ordered(is_upper(bit + 1), near, far)
        gathered = near
        bit += 2
    first, gathered = together(first, gathered)
    wt = gathered.reshape(model, 3 * width + 64).T
    late = send(first, lambda d, z: None if at_home(d, z) else (d, z ^ 1))
    first_other = send(first, other_core)

    pack = jnp.concatenate(
        [hidden_down]
        + [hidden_up[:, k * model : (k + 1) * model] for k in range(groups)]
        + [attend_out]
    )
    height = pack.shape[0]
    weights = lax.all_gather(pack, "dp", axis=0, tiled=False)
    split = dp if (model // dp) % 96 == 0 else 1
    if split == 1:
        tall = hidden_down.shape[0]
        down = weights[:, :tall].reshape(1, dp * tall, model)
        others = weights[:, tall:].reshape(dp, groups + 1, share, model).transpose(1, 0, 2, 3)
        weights = jnp.concatenate([down, others.reshape(1, -1, model)], axis=1)

    stay_flag = stays.astype(jnp.int32)
    early = jnp.where(stays, member, member ^ 2)
    info = jnp.stack([stay_flag, member, core]).astype(jnp.int32)
    info_early = jnp.stack([stay_flag, early, early ^ 1, early ^ 2]).astype(jnp.int32)
    info_late = jnp.stack([stay_flag, early ^ 3]).astype(jnp.int32)
    carried = project(
        info_early, [mine, mine_other, first, first_other, first_other, first], wt, None
    )
    late, packed, grad_mine = together(late, carried[0], cotangent[0])
    late_other = send(late, other_core)
    packed, normed = project(info_late, [late_other, late], wt, [packed, carried[1]])
    grad_moved = send(grad_mine, swap)

    *outs, logsum = attend_forward(info, packed)
    mine, first, logsum = together(mine, first, logsum)
    routes = [None, next_chip, other_core, lambda d, z: (d ^ 1, z ^ 1)]
    merged = [outs[0]] + [send(outs[j], routes[j]) for j in (1, 3, 2)]
    merged = [merged[0], merged[1], merged[3], merged[2]]

    tokens = jnp.where(stays, mine, first)
    cot = jnp.where(stays, grad_mine, grad_moved)
    layer_out, resid_grad, a0, a1, a2, a3, stats, down_own, down_other, grads = hidden_layer(
        info, tokens, cot, merged, wt, weights, groups
    )
    r1 = send(a1, routes[1])
    r3 = send(a3, routes[3])
    r2 = send(a2, routes[2])
    if split == 1:
        grads = grads[0].reshape(groups + 1, dp, share, model).transpose(1, 0, 2, 3)
        grads = grads.reshape(dp, (groups + 1) * share, model)
        down_pieces = [
            lax.psum_scatter(
                down_own.reshape(dp, -1, model), "dp", scatter_dimension=0, tiled=True
            )[0]
        ]
    else:
        down_got = send(down_other, other_core)
        chip = row >> 1

        def down_piece(j):
            mine_at = [
                lax.dynamic_index_in_dim(v, chip ^ j, 0, keepdims=False).astype(F32)
                for v in (down_own, down_got)
            ]
            return (mine_at[0] + mine_at[1]).astype(BF)

        down_pieces = [down_piece(0)]
        down_pieces += [send(down_piece(j), flipped(j << 1)) for j in range(1, dp // 2)]
    reduced = lax.psum_scatter(grads, "dp", scatter_dimension=0, tiled=True)[0]

    layer_out, r3 = together(layer_out, r3)
    layer_moved = send(layer_out, swap)
    def to_owner(value, owner):
        return send(value, lambda d, z: None if (d & 1) == owner else (d ^ 1, z))

    def to_chip(value, owner):
        return send(value, lambda d, z: (d, z ^ 1) if (d & 1) == owner else None)

    def home_from(owner):
        return lambda d, z: None if at_home(d, z) or (d & 1) != owner else (d ^ 1, z ^ 2)

    all_grads = [a0, r1, r2, r3]
    near, far, stacked, *state = attend_backward(info, packed, outs, all_grads, logsum, wt)
    near, far, layer_moved, *down_pieces = together(near, far, layer_moved, *down_pieces)
    down_sum = sum([p.astype(F32) for p in down_pieces[1:]], down_pieces[0].astype(F32))
    down_sum = down_sum.astype(BF)
    far_other, near_other = to_owner(far, 1), to_owner(near, 1)
    partial = (far.astype(F32) + far_other.astype(F32)).astype(BF)
    partial, stacked = together(partial, stacked)
    far_chip = to_chip(partial, 1)
    dw = project_grad(stacked, normed, 1)
    state[0], dw, reduced = together(state[0], dw, reduced)
    reduced = jnp.concatenate([down_sum, reduced])
    scattered = lax.psum_scatter(reduced, "seq", scatter_dimension=0, tiled=True)
    near_b, far_b, stacked = attend_backward(
        info, packed, outs, all_grads, logsum, wt, state
    )
    far_chip, far_b, near_b = together(far_chip, far_b, near_b)
    far_b_other, near_b_other = to_owner(far_b, 0), to_owner(near_b, 0)
    far_b_other, scattered = together(far_b_other, scattered)
    partial = (far_b.astype(F32) + far_b_other.astype(F32)).astype(BF)
    partial, stacked, far_chip = together(partial, stacked, far_chip)
    far_b_chip = to_chip(partial, 0)
    input_grad, low_a, stats = final_norm(
        1, info, tokens, [near, near_other, far_chip], resid_grad, wt, stats
    )
    dw = project_grad(stacked, normed, 0, dw)
    far_b_chip, scattered, low_a, dw = together(far_b_chip, scattered, low_a, dw)
    moved_a = send(low_a, home_from(1))
    total = lax.all_gather(scattered, "seq", axis=0, tiled=True)
    input_grad, low_b, stats = final_norm(
        0, info, tokens, [near_b, near_b_other, far_b_chip], resid_grad, wt, stats, input_grad
    )
    moved_b = send(low_b, home_from(0))

    small = jnp.pad(stats.T, ((0, 0), (0, 56))).astype(BF)
    current = jnp.concatenate([dw, small], axis=1).reshape(dp, share, 3 * width + 64)
    top = bits - 1
    while top > 0:
        width_bits = 2 if top > 1 else 1
        quarter = current.shape[0] >> width_bits
        low_bit = top - width_bits + 1
        mine_at = (row >> low_bit) & ((1 << width_bits) - 1)

        def piece(j):
            return lax.dynamic_slice_in_dim(current, (mine_at ^ j) * quarter, quarter, 0)

        pieces = [piece(0)]
        pieces += [send(piece(j), flipped(j << low_bit)) for j in range(1, 1 << width_bits)]
        moved_a, *pieces = together(moved_a, *pieces)
        summed = sum([p.astype(F32) for p in pieces[1:]], pieces[0].astype(F32))
        current = summed.astype(BF)
        top -= width_bits
    got = send(current, lambda d, z: (d, z ^ 2))
    got, moved_b, total = together(got, moved_b, total)
    input_moved = jnp.where(core == 0, moved_a, moved_b)
    current = (current.astype(F32) + got.astype(F32)).astype(BF)
    upper = core == 1
    give = jnp.where(upper, current[0], current[1])
    keep = jnp.where(upper, current[1], current[0])
    got = send(give, other_core)
    pair = jnp.where(upper, jnp.stack([got, keep]), jnp.stack([keep, got]))
    far = send(pair, next_chip)
    odd = (line & 1) == 1
    quad = [
        jnp.where(odd, far[0], pair[0]),
        jnp.where(odd, pair[0], far[0]),
        jnp.where(odd, far[1], pair[1]),
        jnp.where(odd, pair[1], far[1]),
    ]
    proj_grad = jnp.concatenate(
        [q[:, p * width : (p + 1) * width] for p in range(3) for q in quad], axis=1
    ).astype(F32)
    small = sum([q[:, 3 * width :].astype(F32) for q in quad[1:]], quad[0][:, 3 * width :].astype(F32))
    small = small.T
    total = total.astype(F32)

    tall = hidden_down.shape[0]
    down_grad = total[:tall]
    up_grad = jnp.concatenate(
        [total[tall + k * share : tall + (k + 1) * share] for k in range(groups)], axis=1
    )
    out_grad = total[tall + groups * share :]
    return (
        jnp.where(stays, layer_out, layer_moved)[None],
        jnp.where(stays, input_grad, input_moved.astype(F32))[None],
        small[4],
        small[2],
        small[3],
        proj_grad,
        out_grad,
        small[0],
        small[1],
        up_grad,
        down_grad,
    )


def solution(mesh):
    vector, matrix, tokens = P("dp"), P("dp", None), P("dp", "seq", None)
    return jax.shard_map(
        functools.partial(on_device, mesh.shape["dp"]),
        mesh=mesh,
        in_specs=(
            tokens,
            vector,
            vector,
            vector,
            matrix,
            matrix,
            vector,
            vector,
            matrix,
            matrix,
            tokens,
        ),
        out_specs=(
            tokens,
            tokens,
            vector,
            vector,
            vector,
            matrix,
            matrix,
            vector,
            vector,
            matrix,
            matrix,
        ),
        check_vma=False,
    )
```
